32 devices in a mesh: seq: 2 (over x), exp: 16 (over z, y, core).
Axes of the slice: x: 2, y: 2, z: 4, core: 2. Of those that a mesh axis runs over, the one named last changes fastest.
Arguments:
- queries: bfloat16 [2048, 64, 576], P('seq', 'exp'), may hold values from -68 to 68
- keys: bfloat16 [2048, 576], P(('seq', 'exp')), may hold values from -4.5 to 4.5
- block_mask: int32 [4, 4, 8], replicated, may hold values from 0 to 1, as said below
- summary_start: int32 [4], replicated, may hold values from 0 to 448, as said below
Outputs:
- context: bfloat16 [2048, 64, 512], P('seq', 'exp')
The draws below stay inside these ranges and needn't reach their ends.
Inputs may be any that keep to these rules, and one draw needn't show every extreme that they name: block_mask[c, i, i] is 1, entries of own blocks j > i are 0, and entry 4 + c (the candidate's own summary) is 0. `summary_start`: every value is a multiple of 64.
All inputs are finite; a program needn't handle non-finite values.
Results may differ from the reference program's by a relative error of at most 0.0035.
Values may be sent and summed in bfloat16 or wider, within the bound.
No kernel may reach another device: no remote copies, remote signals or barrier semaphores. Data moves between devices by JAX's collectives and lax.ppermute only.
A program may use at most 64 MiB of HBM per device.

```python
import jax
import jax.numpy as jnp
from jax import lax

HEADS = 64
LAT = 512
QK = 576
NBLK = 4
LEN = 512
CAND = 4
BLK = 128
SUMLEN = 64
TOKENS = 2048


def make_keys(key):
    normal_keys = jax.random.normal(jax.random.fold_in(key, 11), (TOKENS, QK), jnp.float32)
    return jnp.clip(normal_keys, -4.5, 4.5)


def draw_keys(key, part):
    return make_keys(key).astype(jnp.bfloat16)


def draw_queries(key, part):
    query_key = jax.random.fold_in(key, 23)
    normal_draw = jax.random.normal(query_key, (TOKENS, HEADS, QK), jnp.float32)
    return jnp.clip(normal_draw, -6.0, 6.0).astype(jnp.bfloat16)


def draw_block_mask(key, part):
    density = jax.random.randint(jax.random.fold_in(key, 31), (CAND, 1, 1), 1, 4)
    raw_draw = jax.random.randint(jax.random.fold_in(key, 32), (CAND, NBLK, NBLK + CAND), 0, 4)
    chosen = (raw_draw < density).astype(jnp.int32)
    block_row = jnp.arange(NBLK)[None, :, None]
    block_col = jnp.arange(NBLK + CAND)[None, None, :]
    cand_index = jnp.arange(CAND)[:, None, None]
    own_part = block_col < NBLK
    result = jnp.where(own_part & (block_col == block_row), 1, jnp.where(own_part & (block_col > block_row), 0, jnp.where(block_col == NBLK + cand_index, 0, chosen)))
    return result.astype(jnp.int32)


def draw_summary_start(key, part):
    slot_count = LEN // SUMLEN
    raw_draw = jax.random.randint(jax.random.fold_in(key, 41), (CAND,), 0, slot_count)
    zero_slot = jax.random.randint(jax.random.fold_in(key, 42), (), 0, CAND)
    last_slot = (zero_slot + 1 + jax.random.randint(jax.random.fold_in(key, 43), (), 0, CAND - 1)) % CAND
    slot_index = jnp.arange(CAND)
    raw_draw = jnp.where(slot_index == zero_slot, 0, jnp.where(slot_index == last_slot, slot_count - 1, raw_draw))
    return (raw_draw * SUMLEN).astype(jnp.int32)


def setup_inputs(seed: int = 0) -> dict:
    streams_of = jax.random.split(jax.random.key(seed), 5)
    return {
        "queries": draw_queries(jax.random.fold_in(streams_of[4], 71), 0),
        "keys": draw_keys(jax.random.fold_in(streams_of[4], 71), 0),
        "block_mask": draw_block_mask(jax.random.fold_in(streams_of[4], 71), 0),
        "summary_start": draw_summary_start(jax.random.fold_in(streams_of[4], 71), 0),
    }


score_scale = 192.0 ** -0.5
neg_big = -1.0e30


def summary_rows(keys, summary_start):
    def take_block(candidate):
        first_row = candidate * LEN + summary_start[candidate]
        return lax.dynamic_slice_in_dim(keys, first_row.astype(jnp.int32), SUMLEN, 0)
    return lax.map(take_block, jnp.arange(CAND, dtype=jnp.int32))


def reference(queries, keys, block_mask, summary_start):
    summaries = summary_rows(keys, summary_start).reshape(CAND * SUMLEN, QK)
    summary_cand = jnp.arange(CAND * SUMLEN, dtype=jnp.int32) // SUMLEN
    positions = jnp.arange(LEN, dtype=jnp.int32)

    def one_candidate(candidate):
        query_rows = lax.dynamic_slice_in_dim(queries, (candidate * LEN).astype(jnp.int32), LEN, 0).astype(jnp.float32)
        own_keys = lax.dynamic_slice_in_dim(keys, (candidate * LEN).astype(jnp.int32), LEN, 0)
        all_keys = jnp.concatenate([own_keys, summaries], axis=0).astype(jnp.float32)
        mask_rows = jnp.take(block_mask[candidate], positions // BLK, axis=0)
        own_ok = (positions[None, :] <= positions[:, None]) & (jnp.take(mask_rows, positions // BLK, axis=1) == 1)
        summary_ok = jnp.take(mask_rows, NBLK + summary_cand, axis=1) == 1
        allowed = jnp.concatenate([own_ok, summary_ok], axis=1)
        scores = jnp.einsum('rhd,kd->rhk', query_rows, all_keys) * score_scale
        scores = jnp.where(allowed[:, None, :], scores, neg_big)
        row_max = jnp.max(scores, axis=2, keepdims=True)
        weights = jnp.where(allowed[:, None, :], jnp.exp(scores - row_max), 0.0)
        row_sum = jnp.sum(weights, axis=2)
        rounded = lax.optimization_barrier(weights.astype(jnp.bfloat16)).astype(jnp.float32)
        numerator = jnp.einsum('rhk,kd->rhd', rounded, all_keys[:, :LAT])
        return (numerator / row_sum[..., None]).astype(jnp.bfloat16)

    result = lax.map(one_candidate, jnp.arange(CAND, dtype=jnp.int32))
    return result.reshape(TOKENS, HEADS, LAT)
```

```python
import functools
import math

import jax
import jax.numpy as jnp
from jax import lax
from jax.experimental import pallas as pl
from jax.experimental.pallas import tpu as pltpu
from jax.sharding import PartitionSpec as P

ROPE = 64
NBLK = 4
TILE = 256

score_scale = 192.0 ** (-0.5) * math.log2(math.e)
neg_big = -1e30


def step_orders(count):
    bits = [1 << k for k in range(1, count.bit_length() - 1)]
    bits.reverse()
    first = bits[:1] + bits[:0:-1]
    return first, first[-1:] + first[:-1]


def slot_offsets(order):
    offsets = [0]
    for bit in order:
        offsets = offsets + [o ^ bit for o in offsets]
    return offsets


def gather_steps(keys):
    count = lax.axis_size("exp")
    first, second = step_orders(count)
    held = keys
    for bit_a, bit_b in zip(first, second):
        pairs = [(i, i ^ (bit_b if i & 1 else bit_a)) for i in range(count)]
        held = jnp.concatenate([held, lax.ppermute(held, "exp", pairs)], axis=0)
    other = lax.ppermute(held, "exp", [(i, i ^ 1) for i in range(count)])
    return held, other


def order_kernel(cpg, offsets_a, offsets_b, start_ref, held_ref, other_ref, keys_ref, own_ref):
    me = lax.axis_index("exp")
    group = lax.axis_index("seq")
    part = me % 2
    shard = held_ref.shape[0] // len(offsets_a)
    for s, (a, b) in enumerate(zip(offsets_a, offsets_b)):
        rows = slice(s * shard, (s + 1) * shard)
        here = (me ^ jnp.where(part == 0, a, b)) * shard
        there = (me ^ 1 ^ jnp.where(part == 0, b, a)) * shard
        keys_ref[pl.ds(pl.multiple_of(here, shard), shard), :] = held_ref[rows, :]
        keys_ref[pl.ds(pl.multiple_of(there, shard), shard), :] = other_ref[rows, :]
    summ = own_ref.shape[0] // cpg
    length = keys_ref.shape[0] // cpg
    for member in range(cpg):
        row = member * length + start_ref[group * cpg + member]
        own_ref[member * summ : (member + 1) * summ, :] = keys_ref[
            pl.ds(pl.multiple_of(row, summ), summ), :
        ]


def attend_kernel(dims, mask_ref, q_ref, keys_ref, sums_ref, out_ref, near, staged, sem):
    heads, cpg, cands, length, block, summ, lat = dims
    width = q_ref.shape[2]
    group = lax.axis_index("seq")
    steps = cpg * NBLK
    near[...] = jnp.zeros_like(near)

    def out_copy(i, slot):
        return pltpu.make_async_copy(
            staged.at[slot], out_ref.at[pl.ds(i * block, block)], sem.at[slot]
        )

    def step(i, _):
        slot = lax.rem(i, 2)
        member, b = i // NBLK, lax.rem(i, NBLK)
        base = ((group * cpg + member) * NBLK + b) * (NBLK + cands)
        near[0:block, :] = keys_ref[pl.ds(pl.multiple_of(i * block, block), block), :]
        n = jnp.int32(block)
        for j in range(NBLK - 1):
            seen = jnp.logical_and(j < b, mask_ref[base + j] == 1)

            @pl.when(seen)
            def _():
                near[pl.ds(pl.multiple_of(n, summ), block), :] = keys_ref[
                    pl.ds(pl.multiple_of(member * length + j * block, block), block), :
                ]

            n = n + jnp.where(seen, block, 0)
        for d in range(cands):
            seen = mask_ref[base + NBLK + d] == 1
            row = ((group ^ (d // cpg)) * cpg + d % cpg) * summ

            @pl.when(seen)
            def _():
                near[pl.ds(pl.multiple_of(n, summ), summ), :] = sums_ref[
                    pl.ds(pl.multiple_of(row, summ), summ), :
                ]

            n = n + jnp.where(seen, summ, 0)
        tiles = (n + TILE - 1) // TILE

        @pl.when(i >= 2)
        def _():
            out_copy(i - 2, slot).wait()

        def attend(tile_total):
            total = TILE * tile_total
            rows = heads * block
            q = q_ref[:, pl.ds(pl.multiple_of(i * block, block), block), :].reshape(rows, width)
            scores = lax.dot_general(
                q, near[:total, :], (((1,), (1,)), ((), ())), preferred_element_type=jnp.float32
            )
            pos = lax.rem(lax.broadcasted_iota(jnp.int32, (rows, 1), 0), block)
            col = lax.broadcasted_iota(jnp.int32, (1, total), 1)
            least = jnp.where(col < block, col, jnp.where(col < n, -1, block))
            scores = jnp.where(least <= pos, scores * score_scale, neg_big)
            weights = jnp.exp2(scores - jnp.max(scores, axis=1, keepdims=True))
            weight_sum = jnp.sum(weights, axis=1, keepdims=True)
            numerator = lax.dot_general(
                weights.astype(jnp.bfloat16),
                near[:total, :lat],
                (((1,), (0,)), ((), ())),
                preferred_element_type=jnp.float32,
            )
            result = (numerator * (1.0 / weight_sum)).astype(jnp.bfloat16)
            staged[slot] = jnp.swapaxes(result.reshape(heads, block, lat), 0, 1)

        for tile_total in range(1, near.shape[0] // TILE + 1):
            pl.when(tiles == tile_total)(functools.partial(attend, tile_total))
        out_copy(i, slot).start()
        return 0

    lax.fori_loop(0, steps, step, 0)
    for i in range(max(steps - 2, 0), steps):
        out_copy(i, i % 2).wait()


def shards(queries, keys, block_mask, summary_start):
    row_total, head_count, key_width = queries.shape
    lat_width = key_width - ROPE
    seq_count = lax.axis_size("seq")
    total_cands = block_mask.shape[0]
    cpg = total_cands // seq_count
    seq_len = row_total // cpg
    block_len = seq_len // NBLK
    summ_len = block_len // 2
    most = NBLK * block_len + (total_cands - 1) * summ_len
    most = -(-most // TILE) * TILE
    vmem = pl.BlockSpec(memory_space=pltpu.VMEM)
    smem = pl.BlockSpec(memory_space=pltpu.SMEM)

    by_head = jnp.transpose(queries, (1, 0, 2))
    held, other = gather_steps(keys)
    first, second = step_orders(lax.axis_size("exp"))
    ordered, own = pl.pallas_call(
        functools.partial(order_kernel, cpg, slot_offsets(first), slot_offsets(second)),
        out_shape=[
            jax.ShapeDtypeStruct((row_total, key_width), keys.dtype),
            jax.ShapeDtypeStruct((cpg * summ_len, key_width), keys.dtype),
        ],
        in_specs=[smem, vmem, vmem],
        out_specs=[vmem, vmem],
        name="order",
    )(summary_start, held, other)
    sums = own
    bit = 1
    while bit < seq_count:
        pairs = [(i, i ^ bit) for i in range(seq_count)]
        sums = jnp.concatenate([sums, lax.ppermute(sums, "seq", pairs)], axis=0)
        bit *= 2
    dims = (head_count, cpg, total_cands, seq_len, block_len, summ_len, lat_width)
    return pl.pallas_call(
        functools.partial(attend_kernel, dims),
        out_shape=jax.ShapeDtypeStruct((row_total, head_count, lat_width), queries.dtype),
        in_specs=[smem, vmem, vmem, vmem],
        out_specs=pl.BlockSpec(memory_space=pl.ANY),
        scratch_shapes=[
            pltpu.VMEM((most, key_width), keys.dtype),
            pltpu.VMEM((2, block_len, head_count, lat_width), queries.dtype),
            pltpu.SemaphoreType.DMA((2,)),
        ],
        compiler_params=pltpu.CompilerParams(vmem_limit_bytes=24 << 20),
        name="attend",
    )(block_mask.reshape(-1), by_head, ordered, sums)


def solution(mesh):
    placed = (P("seq", "exp", None), P(("seq", "exp"), None), P(), P())
    return jax.shard_map(
        shards, mesh=mesh, in_specs=placed, out_specs=P("seq", "exp", None), check_vma=False
    )
```

```python
import functools
import math

import jax
import jax.numpy as jnp
from jax import lax
from jax.experimental import pallas as pl
from jax.experimental.pallas import tpu as pltpu
from jax.sharding import PartitionSpec as P

ROPE = 64
NBLK = 4
TILE = 256

score_scale = 192.0 ** (-0.5) * math.log2(math.e)
neg_big = -1e30


def step_orders(count):
    bits = [1 << k for k in range(1, count.bit_length() - 1)]
    bits.reverse()
    first = bits[:1] + bits[:0:-1]
    return first, first[-1:] + first[:-1]


def slot_offsets(order):
    offsets = [0]
    for bit in order:
        offsets = offsets + [o ^ bit for o in offsets]
    return offsets


def grant(mib):
    return pltpu.CompilerParams(vmem_limit_bytes=mib << 20)


def join_kernel(first_ref, second_ref, out_ref):
    half = first_ref.shape[0]
    out_ref[:half] = first_ref[...]
    out_ref[half:] = second_ref[...]


def join(first, second):
    vmem = pl.BlockSpec(memory_space=pltpu.VMEM)
    return pl.pallas_call(
        join_kernel,
        out_shape=jax.ShapeDtypeStruct((2 * first.shape[0],) + first.shape[1:], first.dtype),
        in_specs=[vmem, vmem],
        out_specs=vmem,
        compiler_params=grant(2),
        name="join",
    )(first, second)


def turn_kernel(in_ref, out_ref):
    for h in range(in_ref.shape[0]):
        out_ref[h] = in_ref[h].T


def turn(by_width, head, total):
    _, width, rows = by_width.shape
    cut = min(rows, 256)
    return pl.pallas_call(
        turn_kernel,
        out_shape=jax.ShapeDtypeStruct((total, rows, width), by_width.dtype),
        grid=(total, rows // cut),
        in_specs=[pl.BlockSpec((1, width, cut), lambda h, i: (head + h, 0, i))],
        out_specs=pl.BlockSpec((1, cut, width), lambda h, i: (h, i, 0)),
        compiler_params=grant(4),
        name="turn",
    )(by_width)


def gather_steps(keys, queries):
    count = lax.axis_size("exp")
    heads = queries.shape[1]
    first, second = step_orders(count)
    last = len(first)
    by_width = jnp.transpose(queries, (1, 2, 0))
    by_head = []
    done = 0
    held = keys[None]
    for k, (bit_a, bit_b) in enumerate(zip(first, second)):
        pairs = [(i, i ^ (bit_b if i & 1 else bit_a)) for i in range(count)]
        got = lax.ppermute(held, "exp", pairs)
        due = heads if k == last - 1 else heads * (k + 1) // (last + 1)
        if due > done:
            piece = turn(by_width, done, due - done)
            got, piece = lax.optimization_barrier((got, piece))
            by_head.append(piece)
            done = due
        held = join(held, got)
    other = lax.ppermute(held, "exp", [(i, i ^ 1) for i in range(count)])
    return held, other, by_head


def order_kernel(cpg, offsets_a, offsets_b, start_ref, held_ref, other_ref, keys_ref, own_ref):
    me = lax.axis_index("exp")
    group = lax.axis_index("seq")
    part = me % 2
    shard = held_ref.shape[1]
    for s, (a, b) in enumerate(zip(offsets_a, offsets_b)):
        here = (me ^ jnp.where(part == 0, a, b)) * shard
        there = (me ^ 1 ^ jnp.where(part == 0, b, a)) * shard
        keys_ref[pl.ds(pl.multiple_of(here, shard), shard), :] = held_ref[s]
        keys_ref[pl.ds(pl.multiple_of(there, shard), shard), :] = other_ref[s]
    summ = own_ref.shape[0] // cpg
    length = keys_ref.shape[0] // cpg
    for member in range(cpg):
        row = member * length + start_ref[group * cpg + member]
        own_ref[member * summ : (member + 1) * summ, :] = keys_ref[
            pl.ds(pl.multiple_of(row, summ), summ), :
        ]


def attend_kernel(dims, mask_ref, keys_ref, sums_ref, *refs):
    heads, cpg, cands, length, block, summ, lat = dims
    q_refs, (out_ref, near, staged, sem) = refs[:-4], refs[-4:]
    group = lax.axis_index("seq")
    steps = cpg * NBLK
    near[...] = jnp.zeros_like(near)

    def out_copy(i, slot):
        return pltpu.make_async_copy(
            staged.at[slot], out_ref.at[pl.ds(i * block, block)], sem.at[slot]
        )

    def step(i, _):
        slot = lax.rem(i, 2)
        member, b = i // NBLK, lax.rem(i, NBLK)
        cand = group * cpg + member
        near[0:block, :] = keys_ref[pl.ds(pl.multiple_of(i * block, block), block), :]
        n = jnp.int32(block)
        for j in range(NBLK - 1):
            seen = jnp.logical_and(j < b, mask_ref[cand, b, j] == 1)

            @pl.when(seen)
            def _():
                near[pl.ds(pl.multiple_of(n, summ), block), :] = keys_ref[
                    pl.ds(pl.multiple_of(member * length + j * block, block), block), :
                ]

            n = n + jnp.where(seen, block, 0)
        for d in range(cands):
            seen = mask_ref[cand, b, NBLK + d] == 1
            row = ((group ^ (d // cpg)) * cpg + d % cpg) * summ

            @pl.when(seen)
            def _():
                near[pl.ds(pl.multiple_of(n, summ), summ), :] = sums_ref[
                    pl.ds(pl.multiple_of(row, summ), summ), :
                ]

            n = n + jnp.where(seen, summ, 0)
        tiles = (n + TILE - 1) // TILE

        @pl.when(i >= 2)
        def _():
            out_copy(i - 2, slot).wait()

        def attend(tile_total):
            total = TILE * tile_total
            rows = heads * block
            at = pl.ds(pl.multiple_of(i * block, block), block)
            q = jnp.concatenate(
                [q_ref[h, at, :] for q_ref in q_refs for h in range(q_ref.shape[0])], axis=0
            )
            scores = lax.dot_general(
                q, near[:total, :], (((1,), (1,)), ((), ())), preferred_element_type=jnp.float32
            )
            pos = lax.rem(lax.broadcasted_iota(jnp.int32, (rows, 1), 0), block)
            col = lax.broadcasted_iota(jnp.int32, (1, total), 1)
            least = jnp.where(col < block, col, jnp.where(col < n, -1, block))
            scores = jnp.where(least <= pos, scores * score_scale, neg_big)
            weights = jnp.exp2(scores - jnp.max(scores, axis=1, keepdims=True))
            weight_sum = jnp.sum(weights, axis=1, keepdims=True)
            numerator = lax.dot_general(
                weights.astype(jnp.bfloat16),
                near[:total, :lat],
                (((1,), (0,)), ((), ())),
                preferred_element_type=jnp.float32,
            )
            result = (numerator * (1.0 / weight_sum)).astype(jnp.bfloat16)
            staged[slot] = jnp.swapaxes(result.reshape(heads, block, lat), 0, 1)

        for tile_total in range(1, near.shape[0] // TILE + 1):
            pl.when(tiles == tile_total)(functools.partial(attend, tile_total))
        out_copy(i, slot).start()
        return 0

    lax.fori_loop(0, steps, step, 0)
    for i in range(max(steps - 2, 0), steps):
        out_copy(i, i % 2).wait()


def shards(queries, keys, block_mask, summary_start):
    row_total, head_count, key_width = queries.shape
    lat_width = key_width - ROPE
    seq_count = lax.axis_size("seq")
    total_cands = block_mask.shape[0]
    cpg = total_cands // seq_count
    seq_len = row_total // cpg
    block_len = seq_len // NBLK
    summ_len = block_len // 2
    most = NBLK * block_len + (total_cands - 1) * summ_len
    most = -(-most // TILE) * TILE
    vmem = pl.BlockSpec(memory_space=pltpu.VMEM)
    smem = pl.BlockSpec(memory_space=pltpu.SMEM)

    held, other, by_head = gather_steps(keys, queries)
    first, second = step_orders(lax.axis_size("exp"))
    ordered, own = pl.pallas_call(
        functools.partial(order_kernel, cpg, slot_offsets(first), slot_offsets(second)),
        out_shape=[
            jax.ShapeDtypeStruct((row_total, key_width), keys.dtype),
            jax.ShapeDtypeStruct((cpg * summ_len, key_width), keys.dtype),
        ],
        in_specs=[smem, vmem, vmem],
        out_specs=[vmem, vmem],
        compiler_params=grant(4),
        name="order",
    )(summary_start, held, other)
    sums = own
    bit = 1
    while bit < seq_count:
        pairs = [(i, i ^ bit) for i in range(seq_count)]
        sums = join(sums, lax.ppermute(sums, "seq", pairs))
        bit *= 2
    dims = (head_count, cpg, total_cands, seq_len, block_len, summ_len, lat_width)
    return pl.pallas_call(
        functools.partial(attend_kernel, dims),
        out_shape=jax.ShapeDtypeStruct((row_total, head_count, lat_width), queries.dtype),
        in_specs=[smem, vmem, vmem] + [vmem] * len(by_head),
        out_specs=pl.BlockSpec(memory_space=pl.ANY),
        scratch_shapes=[
            pltpu.VMEM((most, key_width), keys.dtype),
            pltpu.VMEM((2, block_len, head_count, lat_width), queries.dtype),
            pltpu.SemaphoreType.DMA((2,)),
        ],
        compiler_params=grant(24),
        name="attend",
    )(block_mask, ordered, sums, *by_head)


def solution(mesh):
    placed = (P("seq", "exp", None), P(("seq", "exp"), None), P(), P())
    return jax.shard_map(
        shards, mesh=mesh, in_specs=placed, out_specs=P("seq", "exp", None), check_vma=False
    )
```

```python
import functools
import math

import jax
import jax.numpy as jnp
from jax import lax
from jax.experimental import pallas as pl
from jax.experimental.pallas import tpu as pltpu
from jax.sharding import PartitionSpec as P

ROPE = 64
NBLK = 4
TILE = 256

score_scale = 192.0 ** (-0.5) * math.log2(math.e)
neg_big = -1e30


def step_orders(count):
    bits = [1 << k for k in range(1, count.bit_length() - 1)]
    bits.reverse()
    first = bits[:1] + bits[:0:-1]
    return first, first[-1:] + first[:-1]


def slot_offsets(order):
    offsets = [0]
    for bit in order:
        offsets = offsets + [o ^ bit for o in offsets]
    return offsets


def grant(mib):
    return pltpu.CompilerParams(vmem_limit_bytes=mib << 20)


def join_kernel(first_ref, second_ref, out_ref):
    half = first_ref.shape[0]
    out_ref[:half] = first_ref[...]
    out_ref[half:] = second_ref[...]


def join(first, second):
    vmem = pl.BlockSpec(memory_space=pltpu.VMEM)
    return pl.pallas_call(
        join_kernel,
        out_shape=jax.ShapeDtypeStruct((2 * first.shape[0],) + first.shape[1:], first.dtype),
        in_specs=[vmem, vmem],
        out_specs=vmem,
        compiler_params=grant(2),
        name="join",
    )(first, second)


def turn_kernel(in_ref, out_ref):
    for h in range(in_ref.shape[0]):
        out_ref[h] = in_ref[h].T


def turn(by_width, head, total):
    _, width, rows = by_width.shape
    cut = min(rows, 256)
    return pl.pallas_call(
        turn_kernel,
        out_shape=jax.ShapeDtypeStruct((total, rows, width), by_width.dtype),
        grid=(total, rows // cut),
        in_specs=[pl.BlockSpec((1, width, cut), lambda h, i: (head + h, 0, i))],
        out_specs=pl.BlockSpec((1, cut, width), lambda h, i: (h, i, 0)),
        compiler_params=grant(4),
        name="turn",
    )(by_width)


def gather_steps(keys, queries):
    count = lax.axis_size("exp")
    heads = queries.shape[1]
    first, second = step_orders(count)
    last = len(first)
    by_width = jnp.transpose(queries, (1, 2, 0))
    by_head = []
    done = 0
    held = keys[None]
    for k, (bit_a, bit_b) in enumerate(zip(first, second)):
        pairs = [(i, i ^ (bit_b if i & 1 else bit_a)) for i in range(count)]
        got = lax.ppermute(held, "exp", pairs)
        due = heads if k == last - 1 else heads * (k + 1) // (last + 1)
        if due > done:
            piece = turn(by_width, done, due - done)
            got, piece = lax.optimization_barrier((got, piece))
            by_head.append(piece)
            done = due
        held = join(held, got)
    other = lax.ppermute(held, "exp", [(i, i ^ 1) for i in range(count)])
    return held, other, by_head


def order_kernel(cpg, offsets_a, offsets_b, start_ref, held_ref, other_ref, keys_ref, own_ref):
    me = lax.axis_index("exp")
    group = lax.axis_index("seq")
    part = me % 2
    shard = held_ref.shape[1]
    for s, (a, b) in enumerate(zip(offsets_a, offsets_b)):
        here = (me ^ jnp.where(part == 0, a, b)) * shard
        there = (me ^ 1 ^ jnp.where(part == 0, b, a)) * shard
        keys_ref[pl.ds(pl.multiple_of(here, shard), shard), :] = held_ref[s]
        keys_ref[pl.ds(pl.multiple_of(there, shard), shard), :] = other_ref[s]
    summ = own_ref.shape[0] // cpg
    length = keys_ref.shape[0] // cpg
    for member in range(cpg):
        row = member * length + start_ref[group * cpg + member]
        own_ref[member * summ : (member + 1) * summ, :] = keys_ref[
            pl.ds(pl.multiple_of(row, summ), summ), :
        ]


def widths(most):
    return list(range(TILE, most, TILE)) + [most]


def queries_at(q_refs, at):
    return jnp.concatenate([q[h, at, :] for q in q_refs for h in range(q.shape[0])], axis=0)


def block_at(i, block):
    return pl.ds(pl.multiple_of(i * block, block), block)


def scores_of(q, keys):
    return score_scale * lax.dot_general(
        q, keys, (((1,), (1,)), ((), ())), preferred_element_type=jnp.float32
    )


def values_of(weights, keys):
    return lax.dot_general(
        weights.astype(jnp.bfloat16),
        keys,
        (((1,), (0,)), ((), ())),
        preferred_element_type=jnp.float32,
    )


def score_kernel(dims, mask_ref, keys_ref, own_ref, *refs):
    heads, cpg, cands, length, block, summ, lat = dims
    q_refs, (scores_ref, most_ref, near_ref) = refs[:-3], refs[-3:]
    group = lax.axis_index("seq")
    rows = heads * block

    def step(i, _):
        member, b = i // NBLK, lax.rem(i, NBLK)
        cand = group * cpg + member
        near_ref[i, 0:block, :] = keys_ref[block_at(i, block), :]
        n = jnp.int32(block)
        for j in range(NBLK - 1):
            seen = jnp.logical_and(j < b, mask_ref[cand, b, j] == 1)

            @pl.when(seen)
            def _():
                near_ref[i, pl.ds(pl.multiple_of(n, summ), block), :] = keys_ref[
                    pl.ds(pl.multiple_of(member * length + j * block, block), block), :
                ]

            n = n + jnp.where(seen, block, 0)
        for d in range(cpg):
            seen = mask_ref[cand, b, NBLK + group * cpg + d] == 1

            @pl.when(seen)
            def _():
                near_ref[i, pl.ds(pl.multiple_of(n, summ), summ), :] = own_ref[
                    d * summ : (d + 1) * summ, :
                ]

            n = n + jnp.where(seen, summ, 0)
        near_ref[i, pl.ds(pl.multiple_of(n, summ), TILE), :] = jnp.zeros(
            (TILE, near_ref.shape[2]), near_ref.dtype
        )

        def score(total):
            scores = scores_of(queries_at(q_refs, block_at(i, block)), near_ref[i, :total, :])
            pos = lax.rem(lax.broadcasted_iota(jnp.int32, (rows, 1), 0), block)
            col = lax.broadcasted_iota(jnp.int32, (1, total), 1)
            least = jnp.where(col < block, col, jnp.where(col < n, -1, block))
            scores = jnp.where(least <= pos, scores, neg_big)
            scores_ref[i, :, :total] = scores
            most_ref[i] = jnp.max(scores, axis=1, keepdims=True)

        low = 0
        for total in widths(scores_ref.shape[2]):
            pl.when(jnp.logical_and(n > low, n <= total))(functools.partial(score, total))
            low = total
        return 0

    lax.fori_loop(0, cpg * NBLK, step, 0)


def finish_kernel(dims, mask_ref, sums_ref, scores_ref, most_ref, near_ref, *refs):
    heads, cpg, cands, length, block, summ, lat = dims
    q_refs, (out_ref, far, total_ref, part_ref, staged, sem) = refs[:-6], refs[-6:]
    group = lax.axis_index("seq")
    steps = cpg * NBLK
    far[...] = jnp.zeros_like(far)
    total_ref[...] = jnp.zeros_like(total_ref)
    part_ref[...] = jnp.zeros_like(part_ref)

    def out_copy(i, slot):
        return pltpu.make_async_copy(
            staged.at[slot], out_ref.at[pl.ds(i * block, block)], sem.at[slot]
        )

    def put(slot):
        result = (total_ref[...] * part_ref[...]).astype(jnp.bfloat16)
        staged[slot] = jnp.swapaxes(result.reshape(heads, block, lat), 0, 1)

    def step(i, _):
        slot = lax.rem(i + 1, 2)
        member, b = i // NBLK, lax.rem(i, NBLK)
        cand = group * cpg + member
        own_total = jnp.int32(block)
        for j in range(NBLK - 1):
            seen = jnp.logical_and(j < b, mask_ref[cand, b, j] == 1)
            own_total = own_total + jnp.where(seen, block, 0)
        n = jnp.int32(0)
        for d in range(cands):
            seen = mask_ref[cand, b, NBLK + d] == 1
            row = ((group ^ (d // cpg)) * cpg + d % cpg) * summ
            away = jnp.logical_and(seen, d // cpg != group)

            @pl.when(away)
            def _():
                far[pl.ds(pl.multiple_of(n, summ), summ), :] = sums_ref[
                    pl.ds(pl.multiple_of(row, summ), summ), :
                ]

            n = n + jnp.where(away, summ, 0)
            own_total = own_total + jnp.where(jnp.logical_and(seen, d // cpg == group), summ, 0)

        @pl.when(i >= 3)
        def _():
            out_copy(i - 3, slot).wait()

        def finish(total, extra):
            put(slot)
            scores = scores_ref[i, :, :total]
            most = most_ref[i]
            if extra:
                more = scores_of(queries_at(q_refs, block_at(i, block)), far[:extra, :])
                col = lax.broadcasted_iota(jnp.int32, (1, extra), 1)
                more = jnp.where(col < n, more, neg_big)
                most = jnp.maximum(most, jnp.max(more, axis=1, keepdims=True))
            weights = jnp.exp2(scores - most)
            weight_sum = jnp.sum(weights, axis=1, keepdims=True)
            numerator = values_of(weights, near_ref[i, :total, :lat])
            if extra:
                weights = jnp.exp2(more - most)
                weight_sum = weight_sum + jnp.sum(weights, axis=1, keepdims=True)
                numerator = numerator + values_of(weights, far[:extra, :lat])
            total_ref[...] = numerator
            part_ref[...] = 1.0 / weight_sum

        low = 0
        for total in widths(scores_ref.shape[2]):
            fits = jnp.logical_and(own_total > low, own_total <= total)
            low = total
            below = -1
            for extra in [0] + (widths(far.shape[0]) if cands > cpg else []):
                takes = jnp.logical_and(n > below, n <= extra)
                pl.when(jnp.logical_and(fits, takes))(functools.partial(finish, total, extra))
                below = extra

        @pl.when(i >= 1)
        def _():
            out_copy(i - 1, slot).start()

        return 0

    lax.fori_loop(0, steps, step, 0)
    last = (steps + 1) % 2
    if steps >= 3:
        out_copy(steps - 3, last).wait()
    put(last)
    out_copy(steps - 1, last).start()
    if steps >= 2:
        out_copy(steps - 2, 1 - last).wait()
    out_copy(steps - 1, last).wait()


def shards(queries, keys, block_mask, summary_start):
    row_total, head_count, key_width = queries.shape
    lat_width = key_width - ROPE
    seq_count = lax.axis_size("seq")
    total_cands = block_mask.shape[0]
    cpg = total_cands // seq_count
    seq_len = row_total // cpg
    block_len = seq_len // NBLK
    summ_len = block_len // 2
    steps, rows = cpg * NBLK, head_count * block_len
    own_most = -(-(NBLK * block_len + (cpg - 1) * summ_len) // 128) * 128
    far_most = -(-max(total_cands - cpg, 1) * summ_len // 128) * 128
    vmem = pl.BlockSpec(memory_space=pltpu.VMEM)
    smem = pl.BlockSpec(memory_space=pltpu.SMEM)

    held, other, by_head = gather_steps(keys, queries)
    first, second = step_orders(lax.axis_size("exp"))
    ordered, own = pl.pallas_call(
        functools.partial(order_kernel, cpg, slot_offsets(first), slot_offsets(second)),
        out_shape=[
            jax.ShapeDtypeStruct((row_total, key_width), keys.dtype),
            jax.ShapeDtypeStruct((cpg * summ_len, key_width), keys.dtype),
        ],
        in_specs=[smem, vmem, vmem],
        out_specs=[vmem, vmem],
        compiler_params=grant(4),
        name="order",
    )(summary_start, held, other)
    dims = (head_count, cpg, total_cands, seq_len, block_len, summ_len, lat_width)
    scores, most, near = pl.pallas_call(
        functools.partial(score_kernel, dims),
        out_shape=[
            jax.ShapeDtypeStruct((steps, rows, own_most), jnp.float32),
            jax.ShapeDtypeStruct((steps, rows, 1), jnp.float32),
            jax.ShapeDtypeStruct((steps, own_most + TILE, key_width), keys.dtype),
        ],
        in_specs=[smem, vmem, vmem] + [vmem] * len(by_head),
        out_specs=[vmem, vmem, vmem],
        compiler_params=grant(8),
        cost_estimate=pl.CostEstimate(
            flops=2 * steps * rows * own_most * key_width, bytes_accessed=0, transcendentals=0
        ),
        name="score",
    )(block_mask, ordered, own, *by_head)
    sums = own
    bit = 1
    while bit < seq_count:
        pairs = [(i, i ^ bit) for i in range(seq_count)]
        got = lax.ppermute(sums, "seq", pairs)
        if 2 * bit >= seq_count:
            got, scores = lax.optimization_barrier((got, scores))
        sums = join(sums, got)
        bit *= 2
    return pl.pallas_call(
        functools.partial(finish_kernel, dims),
        out_shape=jax.ShapeDtypeStruct((row_total, head_count, lat_width), queries.dtype),
        in_specs=[smem, vmem, vmem, vmem, vmem] + [vmem] * len(by_head),
        out_specs=pl.BlockSpec(memory_space=pl.ANY),
        scratch_shapes=[
            pltpu.VMEM((far_most, key_width), keys.dtype),
            pltpu.VMEM((rows, lat_width), jnp.float32),
            pltpu.VMEM((rows, 1), jnp.float32),
            pltpu.VMEM((2, block_len, head_count, lat_width), queries.dtype),
            pltpu.SemaphoreType.DMA((2,)),
        ],
        compiler_params=grant(12),
        name="finish",
    )(block_mask, sums, scores, most, near, *by_head)


def solution(mesh):
    placed = (P("seq", "exp", None), P(("seq", "exp"), None), P(), P())
    return jax.shard_map(
        shards, mesh=mesh, in_specs=placed, out_specs=P("seq", "exp", None), check_vma=False
    )
```

```python
import functools
import math

import jax
import jax.numpy as jnp
from jax import lax
from jax.experimental import pallas as pl
from jax.experimental.pallas import tpu as pltpu
from jax.sharding import PartitionSpec as P

ROPE = 64
NBLK = 4
TILE = 256

score_scale = 192.0 ** (-0.5) * math.log2(math.e)
neg_big = -1e30


def step_orders(count):
    bits = [1 << k for k in range(1, count.bit_length() - 1)]
    bits.reverse()
    first = bits[:1] + bits[:0:-1]
    return first, first[-1:] + first[:-1]


def slot_offsets(order):
    offsets = [0]
    for bit in order:
        offsets = offsets + [o ^ bit for o in offsets]
    return offsets


def grant(mib):
    return pltpu.CompilerParams(vmem_limit_bytes=mib << 20)


def join_kernel(first_ref, second_ref, out_ref):
    half = first_ref.shape[0]
    out_ref[:half] = first_ref[...]
    out_ref[half:] = second_ref[...]


def join(first, second):
    vmem = pl.BlockSpec(memory_space=pltpu.VMEM)
    return pl.pallas_call(
        join_kernel,
        out_shape=jax.ShapeDtypeStruct((2 * first.shape[0],) + first.shape[1:], first.dtype),
        in_specs=[vmem, vmem],
        out_specs=vmem,
        compiler_params=grant(2),
        name="join",
    )(first, second)


def turn_kernel(in_ref, out_ref):
    for h in range(in_ref.shape[0]):
        out_ref[h] = in_ref[h].T


def turn(by_width, head, total):
    _, width, rows = by_width.shape
    cut = min(rows, 256)
    return pl.pallas_call(
        turn_kernel,
        out_shape=jax.ShapeDtypeStruct((total, rows, width), by_width.dtype),
        grid=(total, rows // cut),
        in_specs=[pl.BlockSpec((1, width, cut), lambda h, i: (head + h, 0, i))],
        out_specs=pl.BlockSpec((1, cut, width), lambda h, i: (h, i, 0)),
        compiler_params=grant(4),
        name="turn",
    )(by_width)


def gather_steps(keys, queries):
    count = lax.axis_size("exp")
    heads = queries.shape[1]
    first, second = step_orders(count)
    last = len(first)
    by_width = jnp.transpose(queries, (1, 2, 0))
    by_head = []
    done = 0
    held = keys[None]
    for k, (bit_a, bit_b) in enumerate(zip(first, second)):
        pairs = [(i, i ^ (bit_b if i & 1 else bit_a)) for i in range(count)]
        got = lax.ppermute(held, "exp", pairs)
        due = heads if k == last - 1 else heads * (k + 1) // (last + 1)
        if due > done:
            piece = turn(by_width, done, due - done)
            got, piece = lax.optimization_barrier((got, piece))
            by_head.append(piece)
            done = due
        held = join(held, got)
    other = lax.ppermute(held, "exp", [(i, i ^ 1) for i in range(count)])
    return held, other, by_head


def order_kernel(cpg, offsets_a, offsets_b, start_ref, held_ref, other_ref, keys_ref, own_ref):
    me = lax.axis_index("exp")
    group = lax.axis_index("seq")
    part = me % 2
    shard = held_ref.shape[1]
    for s, (a, b) in enumerate(zip(offsets_a, offsets_b)):
        here = (me ^ jnp.where(part == 0, a, b)) * shard
        there = (me ^ 1 ^ jnp.where(part == 0, b, a)) * shard
        keys_ref[pl.ds(pl.multiple_of(here, shard), shard), :] = held_ref[s]
        keys_ref[pl.ds(pl.multiple_of(there, shard), shard), :] = other_ref[s]
    summ = own_ref.shape[0] // cpg
    length = keys_ref.shape[0] // cpg
    for member in range(cpg):
        row = member * length + start_ref[group * cpg + member]
        own_ref[member * summ : (member + 1) * summ, :] = keys_ref[
            pl.ds(pl.multiple_of(row, summ), summ), :
        ]


def attend_kernel(dims, mask_ref, keys_ref, sums_ref, *refs):
    heads, cpg, cands, length, block, summ, lat = dims
    q_refs, (out_ref, near, total_ref, part_ref, staged, sem) = refs[:-6], refs[-6:]
    group = lax.axis_index("seq")
    rows = heads * block
    near[...] = jnp.zeros_like(near)

    def out_copy(b, member, slot):
        at = pl.ds(pl.multiple_of(member * length + b * block, block), block)
        return pltpu.make_async_copy(
            staged.at[slot, member], out_ref.at[at], sem.at[slot, member]
        )

    def put(slot):
        for member in range(cpg):
            result = (total_ref[member] * part_ref[member]).astype(jnp.bfloat16)
            staged[slot, member] = jnp.swapaxes(result.reshape(heads, block, lat), 0, 1)

    def gather_seen(b, member):
        cand = group * cpg + member
        near[member, 0:block, :] = keys_ref[
            pl.ds(pl.multiple_of(member * length + b * block, block), block), :
        ]
        n = jnp.int32(block)
        for j in range(NBLK - 1):
            seen = jnp.logical_and(j < b, mask_ref[cand, b, j] == 1)

            @pl.when(seen)
            def _():
                near[member, pl.ds(pl.multiple_of(n, summ), block), :] = keys_ref[
                    member * length + j * block : member * length + (j + 1) * block, :
                ]

            n = n + jnp.where(seen, block, 0)
        for d in range(cands):
            seen = mask_ref[cand, b, NBLK + d] == 1
            row = ((group ^ (d // cpg)) * cpg + d % cpg) * summ

            @pl.when(seen)
            def _():
                near[member, pl.ds(pl.multiple_of(n, summ), summ), :] = sums_ref[
                    pl.ds(pl.multiple_of(row, summ), summ), :
                ]

            n = n + jnp.where(seen, summ, 0)
        return n

    def step(b, _):
        slot = lax.rem(b + 1, 2)
        counts = [gather_seen(b, member) for member in range(cpg)]
        tiles = (functools.reduce(jnp.maximum, counts) + TILE - 1) // TILE

        @pl.when(b >= 3)
        def _():
            for member in range(cpg):
                out_copy(b - 3, member, slot).wait()

        def attend(tile_total):
            total = TILE * tile_total
            put(slot)
            all_scores = []
            for member in range(cpg):
                at = pl.ds(pl.multiple_of(member * length + b * block, block), block)
                q = jnp.concatenate(
                    [q_ref[h, at, :] for q_ref in q_refs for h in range(q_ref.shape[0])], axis=0
                )
                all_scores.append(
                    lax.dot_general(
                        q,
                        near[member, :total, :],
                        (((1,), (1,)), ((), ())),
                        preferred_element_type=jnp.float32,
                    )
                )
            pos = lax.rem(lax.broadcasted_iota(jnp.int32, (rows, block), 0), block)
            causal = lax.broadcasted_iota(jnp.int32, (rows, block), 1) <= pos
            col = lax.broadcasted_iota(jnp.int32, (1, total - block), 1) + block
            for member, scores in enumerate(all_scores):
                bias = jnp.where(col < counts[member], 0.0, neg_big)
                first = jnp.where(causal, scores[:, :block] * score_scale, neg_big)
                rest = scores[:, block:] * score_scale + bias
                most = jnp.maximum(
                    jnp.max(first, axis=1, keepdims=True), jnp.max(rest, axis=1, keepdims=True)
                )
                weights = jnp.exp2(jnp.concatenate([first, rest], axis=1) - most)
                part_ref[member] = 1.0 / jnp.sum(weights, axis=1, keepdims=True)
                total_ref[member] = lax.dot_general(
                    weights.astype(jnp.bfloat16),
                    near[member, :total, :lat],
                    (((1,), (0,)), ((), ())),
                    preferred_element_type=jnp.float32,
                )

        for tile_total in range(1, near.shape[1] // TILE + 1):
            pl.when(tiles == tile_total)(functools.partial(attend, tile_total))

        @pl.when(b >= 1)
        def _():
            for member in range(cpg):
                out_copy(b - 1, member, slot).start()

        return 0

    lax.fori_loop(0, NBLK, step, 0)
    last = (NBLK + 1) % 2
    for member in range(cpg):
        out_copy(NBLK - 3, member, last).wait()
    put(last)
    for member in range(cpg):
        out_copy(NBLK - 1, member, last).start()
    for member in range(cpg):
        out_copy(NBLK - 2, member, 1 - last).wait()
        out_copy(NBLK - 1, member, last).wait()


def shards(queries, keys, block_mask, summary_start):
    row_total, head_count, key_width = queries.shape
    lat_width = key_width - ROPE
    seq_count = lax.axis_size("seq")
    total_cands = block_mask.shape[0]
    cpg = total_cands // seq_count
    seq_len = row_total // cpg
    block_len = seq_len // NBLK
    summ_len = block_len // 2
    most = NBLK * block_len + (total_cands - 1) * summ_len
    most = -(-most // TILE) * TILE
    vmem = pl.BlockSpec(memory_space=pltpu.VMEM)
    smem = pl.BlockSpec(memory_space=pltpu.SMEM)

    held, other, by_head = gather_steps(keys, queries)
    first, second = step_orders(lax.axis_size("exp"))
    ordered, own = pl.pallas_call(
        functools.partial(order_kernel, cpg, slot_offsets(first), slot_offsets(second)),
        out_shape=[
            jax.ShapeDtypeStruct((row_total, key_width), keys.dtype),
            jax.ShapeDtypeStruct((cpg * summ_len, key_width), keys.dtype),
        ],
        in_specs=[smem, vmem, vmem],
        out_specs=[vmem, vmem],
        compiler_params=grant(4),
        name="order",
    )(summary_start, held, other)
    sums = own
    bit = 1
    while bit < seq_count:
        pairs = [(i, i ^ bit) for i in range(seq_count)]
        sums = join(sums, lax.ppermute(sums, "seq", pairs))
        bit *= 2
    dims = (head_count, cpg, total_cands, seq_len, block_len, summ_len, lat_width)
    return pl.pallas_call(
        functools.partial(attend_kernel, dims),
        out_shape=jax.ShapeDtypeStruct((row_total, head_count, lat_width), queries.dtype),
        in_specs=[smem, vmem, vmem] + [vmem] * len(by_head),
        out_specs=pl.BlockSpec(memory_space=pl.ANY),
        scratch_shapes=[
            pltpu.VMEM((cpg, most, key_width), keys.dtype),
            pltpu.VMEM((cpg, head_count * block_len, lat_width), jnp.float32),
            pltpu.VMEM((cpg, head_count * block_len, 1), jnp.float32),
            pltpu.VMEM((2, cpg, block_len, head_count, lat_width), queries.dtype),
            pltpu.SemaphoreType.DMA((2, cpg)),
        ],
        compiler_params=grant(24),
        name="attend",
    )(block_mask, ordered, sums, *by_head)


def solution(mesh):
    placed = (P("seq", "exp", None), P(("seq", "exp"), None), P(), P())
    return jax.shard_map(
        shards, mesh=mesh, in_specs=placed, out_specs=P("seq", "exp", None), check_vma=False
    )
```

```python
import functools
import math

import jax
import jax.numpy as jnp
from jax import lax
from jax.experimental import pallas as pl
from jax.experimental.pallas import tpu as pltpu
from jax.sharding import PartitionSpec as P

ROPE = 64
NBLK = 4
TILE = 256

score_scale = 192.0 ** (-0.5) * math.log2(math.e)
neg_big = -1e30


def step_orders(count):
    bits = [1 << k for k in range(1, count.bit_length() - 1)]
    bits.reverse()
    first = bits[:1] + bits[:0:-1]
    return first, first[-1:] + first[:-1]


def slot_offsets(order):
    offsets = [0]
    for bit in order:
        offsets = offsets + [o ^ bit for o in offsets]
    return offsets


def grant(mib):
    return pltpu.CompilerParams(vmem_limit_bytes=mib << 20)


def join_kernel(first_ref, second_ref, out_ref):
    half = first_ref.shape[0]
    out_ref[:half] = first_ref[...]
    out_ref[half:] = second_ref[...]


def join(first, second):
    vmem = pl.BlockSpec(memory_space=pltpu.VMEM)
    return pl.pallas_call(
        join_kernel,
        out_shape=jax.ShapeDtypeStruct((2 * first.shape[0],) + first.shape[1:], first.dtype),
        in_specs=[vmem, vmem],
        out_specs=vmem,
        compiler_params=grant(2),
        name="join",
    )(first, second)


def keep_kernel(in_ref, out_ref):
    out_ref[...] = in_ref[...]


def keep(array):
    vmem = pl.BlockSpec(memory_space=pltpu.VMEM)
    return pl.pallas_call(
        keep_kernel,
        out_shape=jax.ShapeDtypeStruct(array.shape, array.dtype),
        in_specs=[vmem],
        out_specs=vmem,
        compiler_params=grant(2),
        name="keep",
    )(array)


def turn_kernel(in_ref, out_ref):
    for h in range(in_ref.shape[0]):
        out_ref[h] = in_ref[h].T


def turn(by_width, head, total):
    _, width, rows = by_width.shape
    cut = min(rows, 256)
    return pl.pallas_call(
        turn_kernel,
        out_shape=jax.ShapeDtypeStruct((total, rows, width), by_width.dtype),
        grid=(total, rows // cut),
        in_specs=[pl.BlockSpec((1, width, cut), lambda h, i: (head + h, 0, i))],
        out_specs=pl.BlockSpec((1, cut, width), lambda h, i: (h, i, 0)),
        compiler_params=grant(4),
        name="turn",
    )(by_width)


def gather_steps(keys, queries):
    count = lax.axis_size("exp")
    heads = queries.shape[1]
    first, second = step_orders(count)
    last = len(first)
    by_width = jnp.transpose(queries, (1, 2, 0))
    by_head = []
    done = 0
    held = keys[None]
    for k, (bit_a, bit_b) in enumerate(zip(first, second)):
        pairs = [(i, i ^ (bit_b if i & 1 else bit_a)) for i in range(count)]
        got = lax.ppermute(held, "exp", pairs)
        if k == 0:
            got, held = lax.optimization_barrier((got, keep(held)))
        due = heads if k == last - 1 else heads * k // (2 * (last - 1))
        if due > done:
            piece = turn(by_width, done, due - done)
            got, piece = lax.optimization_barrier((got, piece))
            by_head.append(piece)
            done = due
        held = join(held, got)
    other = lax.ppermute(held, "exp", [(i, i ^ 1) for i in range(count)])
    return held, other, by_head


def pick_kernel(cpg, orders, start_ref, held_ref, other_ref, own_ref):
    me = lax.axis_index("exp")
    group = lax.axis_index("seq")
    shard = held_ref.shape[1]
    summ = own_ref.shape[0] // cpg
    length = 2 * held_ref.shape[0] * shard // cpg
    piece = min(shard, summ)
    for member in range(cpg):
        for k in range(summ // piece):
            row = member * length + start_ref[group * cpg + member] + k * piece
            owner = row // shard
            inside = pl.multiple_of(lax.rem(row, shard), piece)
            slots = [
                sum(((owner ^ me) // bit % 2) << place for place, bit in enumerate(order))
                for order in orders
            ]
            part = owner % 2
            slot = jnp.where(part == 0, slots[0], slots[1])
            at = slice(member * summ + k * piece, member * summ + (k + 1) * piece)

            @pl.when(part == me % 2)
            def _():
                own_ref[at, :] = held_ref[slot, pl.ds(inside, piece), :]

            @pl.when(part != me % 2)
            def _():
                own_ref[at, :] = other_ref[slot, pl.ds(inside, piece), :]


def order_kernel(offsets_a, offsets_b, held_ref, other_ref, keys_ref):
    me = lax.axis_index("exp")
    part = me % 2
    shard = held_ref.shape[1]
    for s, (a, b) in enumerate(zip(offsets_a, offsets_b)):
        here = (me ^ jnp.where(part == 0, a, b)) * shard
        there = (me ^ 1 ^ jnp.where(part == 0, b, a)) * shard
        keys_ref[pl.ds(pl.multiple_of(here, shard), shard), :] = held_ref[s]
        keys_ref[pl.ds(pl.multiple_of(there, shard), shard), :] = other_ref[s]


def prepare_kernel(dims, mask_ref, keys_ref, own_ref, near_ref):
    heads, cpg, cands, length, block, summ, lat = dims
    group = lax.axis_index("seq")
    tail = (cands - cpg) * summ + TILE

    def step(i, _):
        member, b = i // NBLK, lax.rem(i, NBLK)
        cand = group * cpg + member
        near_ref[i, 0:block, :] = keys_ref[pl.ds(pl.multiple_of(i * block, block), block), :]
        n = jnp.int32(block)
        for j in range(NBLK - 1):
            seen = jnp.logical_and(j < b, mask_ref[cand, b, j] == 1)

            @pl.when(seen)
            def _():
                near_ref[i, pl.ds(pl.multiple_of(n, summ), block), :] = keys_ref[
                    pl.ds(pl.multiple_of(member * length + j * block, block), block), :
                ]

            n = n + jnp.where(seen, block, 0)
        for d in range(cpg):
            seen = mask_ref[cand, b, NBLK + group * cpg + d] == 1

            @pl.when(seen)
            def _():
                near_ref[i, pl.ds(pl.multiple_of(n, summ), summ), :] = own_ref[
                    d * summ : (d + 1) * summ, :
                ]

            n = n + jnp.where(seen, summ, 0)
        near_ref[i, pl.ds(pl.multiple_of(n, summ), tail), :] = jnp.zeros(
            (tail, near_ref.shape[2]), near_ref.dtype
        )
        return 0

    lax.fori_loop(0, cpg * NBLK, step, 0)


def attend_kernel(dims, most, mask_ref, got_ref, sums_ref, *refs):
    heads, cpg, cands, length, block, summ, lat = dims
    q_refs, (out_ref, near, total_ref, part_ref, staged, sem) = refs[:-6], refs[-6:]
    group = lax.axis_index("seq")
    rows = heads * block

    def out_copy(b, member, slot):
        at = pl.ds(pl.multiple_of(member * length + b * block, block), block)
        return pltpu.make_async_copy(
            staged.at[slot, member], out_ref.at[at], sem.at[slot, member]
        )

    def put(slot):
        for member in range(cpg):
            result = (total_ref[member] * part_ref[member]).astype(jnp.bfloat16)
            staged[slot, member] = jnp.swapaxes(result.reshape(heads, block, lat), 0, 1)

    def add_seen(b, member):
        cand = group * cpg + member
        n = jnp.int32(block)
        for j in range(NBLK - 1):
            n = n + jnp.where(jnp.logical_and(j < b, mask_ref[cand, b, j] == 1), block, 0)
        for d in range(cpg):
            n = n + jnp.where(mask_ref[cand, b, NBLK + group * cpg + d] == 1, summ, 0)
        for d in range(cands):
            seen = jnp.logical_and(mask_ref[cand, b, NBLK + d] == 1, d // cpg != group)
            row = ((group ^ (d // cpg)) * cpg + d % cpg) * summ

            @pl.when(seen)
            def _():
                near[member * NBLK + b, pl.ds(pl.multiple_of(n, summ), summ), :] = sums_ref[
                    pl.ds(pl.multiple_of(row, summ), summ), :
                ]

            n = n + jnp.where(seen, summ, 0)
        return n

    def step(b, _):
        slot = lax.rem(b + 1, 2)
        counts = [add_seen(b, member) for member in range(cpg)]
        tiles = (functools.reduce(jnp.maximum, counts) + TILE - 1) // TILE

        @pl.when(b >= 3)
        def _():
            for member in range(cpg):
                out_copy(b - 3, member, slot).wait()

        def attend(tile_total):
            total = TILE * tile_total
            put(slot)
            all_scores = []
            for member in range(cpg):
                at = pl.ds(pl.multiple_of(member * length + b * block, block), block)
                q = jnp.concatenate(
                    [q_ref[h, at, :] for q_ref in q_refs for h in range(q_ref.shape[0])], axis=0
                )
                all_scores.append(
                    lax.dot_general(
                        q,
                        near[member * NBLK + b, :total, :],
                        (((1,), (1,)), ((), ())),
                        preferred_element_type=jnp.float32,
                    )
                )
            pos = lax.rem(lax.broadcasted_iota(jnp.int32, (rows, block), 0), block)
            causal = lax.broadcasted_iota(jnp.int32, (rows, block), 1) <= pos
            col = lax.broadcasted_iota(jnp.int32, (1, total - block), 1) + block
            for member, scores in enumerate(all_scores):
                bias = jnp.where(col < counts[member], 0.0, neg_big)
                first = jnp.where(causal, scores[:, :block] * score_scale, neg_big)
                rest = scores[:, block:] * score_scale + bias
                most = jnp.maximum(
                    jnp.max(first, axis=1, keepdims=True), jnp.max(rest, axis=1, keepdims=True)
                )
                weights = jnp.exp2(jnp.concatenate([first, rest], axis=1) - most)
                part_ref[member] = 1.0 / jnp.sum(weights, axis=1, keepdims=True)
                total_ref[member] = lax.dot_general(
                    weights.astype(jnp.bfloat16),
                    near[member * NBLK + b, :total, :lat],
                    (((1,), (0,)), ((), ())),
                    preferred_element_type=jnp.float32,
                )

        for tile_total in range(1, most // TILE + 1):
            pl.when(tiles == tile_total)(functools.partial(attend, tile_total))

        @pl.when(b >= 1)
        def _():
            for member in range(cpg):
                out_copy(b - 1, member, slot).start()

        return 0

    lax.fori_loop(0, NBLK, step, 0)
    last = (NBLK + 1) % 2
    for member in range(cpg):
        out_copy(NBLK - 3, member, last).wait()
    put(last)
    for member in range(cpg):
        out_copy(NBLK - 1, member, last).start()
    for member in range(cpg):
        out_copy(NBLK - 2, member, 1 - last).wait()
        out_copy(NBLK - 1, member, last).wait()


def shards(queries, keys, block_mask, summary_start):
    row_total, head_count, key_width = queries.shape
    lat_width = key_width - ROPE
    seq_count = lax.axis_size("seq")
    total_cands = block_mask.shape[0]
    cpg = total_cands // seq_count
    seq_len = row_total // cpg
    block_len = seq_len // NBLK
    summ_len = block_len // 2
    most = NBLK * block_len + (total_cands - 1) * summ_len
    most = -(-most // TILE) * TILE
    vmem = pl.BlockSpec(memory_space=pltpu.VMEM)
    smem = pl.BlockSpec(memory_space=pltpu.SMEM)

    held, other, by_head = gather_steps(keys, queries)
    first, second = step_orders(lax.axis_size("exp"))
    own = pl.pallas_call(
        functools.partial(pick_kernel, cpg, (first, second)),
        out_shape=jax.ShapeDtypeStruct((cpg * summ_len, key_width), keys.dtype),
        in_specs=[smem, vmem, vmem],
        out_specs=vmem,
        compiler_params=grant(2),
        name="pick",
    )(summary_start, held, other)
    ordered = pl.pallas_call(
        functools.partial(order_kernel, slot_offsets(first), slot_offsets(second)),
        out_shape=jax.ShapeDtypeStruct((row_total, key_width), keys.dtype),
        in_specs=[vmem, vmem],
        out_specs=vmem,
        compiler_params=grant(2),
        cost_estimate=pl.CostEstimate(flops=10**9, bytes_accessed=0, transcendentals=0),
        name="order",
    )(held, other)
    dims = (head_count, cpg, total_cands, seq_len, block_len, summ_len, lat_width)
    near_rows = NBLK * block_len + (total_cands - 1) * summ_len + TILE
    near = pl.pallas_call(
        functools.partial(prepare_kernel, dims),
        out_shape=jax.ShapeDtypeStruct((cpg * NBLK, near_rows, key_width), keys.dtype),
        in_specs=[smem, vmem, vmem],
        out_specs=vmem,
        compiler_params=grant(2),
        cost_estimate=pl.CostEstimate(flops=10**9, bytes_accessed=0, transcendentals=0),
        name="prepare",
    )(block_mask, ordered, own)
    sums = own
    bit = 1
    while bit < seq_count:
        pairs = [(i, i ^ bit) for i in range(seq_count)]
        got = lax.ppermute(sums, "seq", pairs)
        if 2 * bit >= seq_count:
            got, near = lax.optimization_barrier((got, near))
        sums = join(sums, got)
        bit *= 2
    rows = head_count * block_len
    return pl.pallas_call(
        functools.partial(attend_kernel, dims, most),
        out_shape=[
            jax.ShapeDtypeStruct((row_total, head_count, lat_width), queries.dtype),
            jax.ShapeDtypeStruct(near.shape, near.dtype),
        ],
        in_specs=[smem, vmem, vmem] + [vmem] * len(by_head),
        out_specs=[pl.BlockSpec(memory_space=pl.ANY), vmem],
        scratch_shapes=[
            pltpu.VMEM((cpg, rows, lat_width), jnp.float32),
            pltpu.VMEM((cpg, rows, 1), jnp.float32),
            pltpu.VMEM((2, cpg, block_len, head_count, lat_width), queries.dtype),
            pltpu.SemaphoreType.DMA((2, cpg)),
        ],
        input_output_aliases={1: 1},
        compiler_params=grant(20),
        name="attend",
    )(block_mask, near, sums, *by_head)[0]


def solution(mesh):
    placed = (P("seq", "exp", None), P(("seq", "exp"), None), P(), P())
    return jax.shard_map(
        shards, mesh=mesh, in_specs=placed, out_specs=P("seq", "exp", None), check_vma=False
    )
```

```python
import functools
import itertools
import math

import jax
import jax.numpy as jnp
from jax import lax
from jax.experimental import pallas as pl
from jax.experimental.pallas import tpu as pltpu
from jax.sharding import PartitionSpec as P

ROPE = 64
NBLK = 4
TILE = 256
MOST_BODIES = 9

score_scale = 192.0 ** (-0.5) * math.log2(math.e)
neg_big = -1e30


def step_orders(count):
    bits = [1 << k for k in range(1, count.bit_length() - 1)]
    bits.reverse()
    first = bits[:1] + bits[:0:-1]
    return first, first[-1:] + first[:-1]


def slot_offsets(order):
    offsets = [0]
    for bit in order:
        offsets = offsets + [o ^ bit for o in offsets]
    return offsets


def grant(mib):
    return pltpu.CompilerParams(vmem_limit_bytes=mib << 20)


def join_kernel(first_ref, second_ref, out_ref):
    half = first_ref.shape[0]
    out_ref[:half] = first_ref[...]
    out_ref[half:] = second_ref[...]


def join(first, second):
    vmem = pl.BlockSpec(memory_space=pltpu.VMEM)
    return pl.pallas_call(
        join_kernel,
        out_shape=jax.ShapeDtypeStruct((2 * first.shape[0],) + first.shape[1:], first.dtype),
        in_specs=[vmem, vmem],
        out_specs=vmem,
        compiler_params=grant(2),
        name="join",
    )(first, second)


def keep_kernel(in_ref, out_ref):
    out_ref[...] = in_ref[...]


def keep(array):
    vmem = pl.BlockSpec(memory_space=pltpu.VMEM)
    return pl.pallas_call(
        keep_kernel,
        out_shape=jax.ShapeDtypeStruct(array.shape, array.dtype),
        in_specs=[vmem],
        out_specs=vmem,
        compiler_params=grant(2),
        name="keep",
    )(array)


def turn_kernel(in_ref, out_ref):
    for h in range(in_ref.shape[0]):
        out_ref[h] = in_ref[h].T


def turn(by_width, head, total):
    _, width, rows = by_width.shape
    cut = min(rows, 256)
    return pl.pallas_call(
        turn_kernel,
        out_shape=jax.ShapeDtypeStruct((total, rows, width), by_width.dtype),
        grid=(total, rows // cut),
        in_specs=[pl.BlockSpec((1, width, cut), lambda h, i: (head + h, 0, i))],
        out_specs=pl.BlockSpec((1, cut, width), lambda h, i: (h, i, 0)),
        compiler_params=grant(4),
        name="turn",
    )(by_width)


def gather_steps(keys, queries):
    count = lax.axis_size("exp")
    heads = queries.shape[1]
    first, second = step_orders(count)
    last = len(first)
    by_width = jnp.transpose(queries, (1, 2, 0))
    by_head = []
    done = 0
    held = keys[None]
    for k, (bit_a, bit_b) in enumerate(zip(first, second)):
        pairs = [(i, i ^ (bit_b if i & 1 else bit_a)) for i in range(count)]
        got = lax.ppermute(held, "exp", pairs)
        if k == 0:
            got, held = lax.optimization_barrier((got, keep(held)))
        due = heads if k == last - 1 else heads * k // (2 * (last - 1))
        if due > done:
            piece = turn(by_width, done, due - done)
            got, piece = lax.optimization_barrier((got, piece))
            by_head.append(piece)
            done = due
        held = join(held, got)
    other = lax.ppermute(held, "exp", [(i, i ^ 1) for i in range(count)])
    return held, other, by_head


def pick_kernel(cpg, orders, start_ref, held_ref, other_ref, own_ref):
    me = lax.axis_index("exp")
    group = lax.axis_index("seq")
    shard = held_ref.shape[1]
    summ = own_ref.shape[0] // cpg
    length = 2 * held_ref.shape[0] * shard // cpg
    piece = min(shard, summ)
    for member in range(cpg):
        for k in range(summ // piece):
            row = member * length + start_ref[group * cpg + member] + k * piece
            owner = row // shard
            inside = pl.multiple_of(lax.rem(row, shard), piece)
            slots = [
                sum(((owner ^ me) // bit % 2) << place for place, bit in enumerate(order))
                for order in orders
            ]
            part = owner % 2
            slot = jnp.where(part == 0, slots[0], slots[1])
            at = slice(member * summ + k * piece, member * summ + (k + 1) * piece)

            @pl.when(part == me % 2)
            def _():
                own_ref[at, :] = held_ref[slot, pl.ds(inside, piece), :]

            @pl.when(part != me % 2)
            def _():
                own_ref[at, :] = other_ref[slot, pl.ds(inside, piece), :]


def order_kernel(offsets_a, offsets_b, held_ref, other_ref, keys_ref):
    me = lax.axis_index("exp")
    part = me % 2
    shard = held_ref.shape[1]
    for s, (a, b) in enumerate(zip(offsets_a, offsets_b)):
        here = (me ^ jnp.where(part == 0, a, b)) * shard
        there = (me ^ 1 ^ jnp.where(part == 0, b, a)) * shard
        keys_ref[pl.ds(pl.multiple_of(here, shard), shard), :] = held_ref[s]
        keys_ref[pl.ds(pl.multiple_of(there, shard), shard), :] = other_ref[s]


def prepare_kernel(dims, mask_ref, keys_ref, own_ref, near_ref):
    heads, cpg, cands, length, block, summ, lat = dims
    group = lax.axis_index("seq")
    tail = (cands - cpg) * summ + TILE

    def step(i, _):
        member, b = i // NBLK, lax.rem(i, NBLK)
        cand = group * cpg + member
        near_ref[i, 0:block, :] = keys_ref[pl.ds(pl.multiple_of(i * block, block), block), :]
        n = jnp.int32(block)
        for j in range(NBLK - 1):
            seen = jnp.logical_and(j < b, mask_ref[cand, b, j] == 1)

            @pl.when(seen)
            def _():
                near_ref[i, pl.ds(pl.multiple_of(n, summ), block), :] = keys_ref[
                    pl.ds(pl.multiple_of(member * length + j * block, block), block), :
                ]

            n = n + jnp.where(seen, block, 0)
        for d in range(cpg):
            seen = mask_ref[cand, b, NBLK + group * cpg + d] == 1

            @pl.when(seen)
            def _():
                near_ref[i, pl.ds(pl.multiple_of(n, summ), summ), :] = own_ref[
                    d * summ : (d + 1) * summ, :
                ]

            n = n + jnp.where(seen, summ, 0)
        near_ref[i, pl.ds(pl.multiple_of(n, summ), tail), :] = jnp.zeros(
            (tail, near_ref.shape[2]), near_ref.dtype
        )
        return 0

    lax.fori_loop(0, cpg * NBLK, step, 0)


def attend_kernel(dims, most, mask_ref, got_ref, sums_ref, *refs):
    heads, cpg, cands, length, block, summ, lat = dims
    q_refs, (out_ref, near, total_ref, part_ref, staged, sem) = refs[:-6], refs[-6:]
    group = lax.axis_index("seq")
    rows = heads * block

    def out_copy(b, member, slot):
        at = pl.ds(pl.multiple_of(member * length + b * block, block), block)
        return pltpu.make_async_copy(
            staged.at[slot, member], out_ref.at[at], sem.at[slot, member]
        )

    def put(slot):
        for member in range(cpg):
            result = (total_ref[member] * part_ref[member]).astype(jnp.bfloat16)
            staged[slot, member] = jnp.swapaxes(result.reshape(heads, block, lat), 0, 1)

    def add_seen(b, member):
        cand = group * cpg + member
        n = jnp.int32(block)
        for j in range(NBLK - 1):
            n = n + jnp.where(jnp.logical_and(j < b, mask_ref[cand, b, j] == 1), block, 0)
        for d in range(cpg):
            n = n + jnp.where(mask_ref[cand, b, NBLK + group * cpg + d] == 1, summ, 0)
        for d in range(cands):
            seen = jnp.logical_and(mask_ref[cand, b, NBLK + d] == 1, d // cpg != group)
            row = ((group ^ (d // cpg)) * cpg + d % cpg) * summ

            @pl.when(seen)
            def _():
                near[member * NBLK + b, pl.ds(pl.multiple_of(n, summ), summ), :] = sums_ref[
                    pl.ds(pl.multiple_of(row, summ), summ), :
                ]

            n = n + jnp.where(seen, summ, 0)
        return n

    def step(b, _):
        slot = lax.rem(b + 1, 2)
        counts = [add_seen(b, member) for member in range(cpg)]

        @pl.when(b >= 3)
        def _():
            for member in range(cpg):
                out_copy(b - 3, member, slot).wait()

        def attend(totals):
            put(slot)
            all_scores = []
            for member, total in enumerate(totals):
                at = pl.ds(pl.multiple_of(member * length + b * block, block), block)
                q = jnp.concatenate(
                    [q_ref[h, at, :] for q_ref in q_refs for h in range(q_ref.shape[0])], axis=0
                )
                all_scores.append(
                    lax.dot_general(
                        q,
                        near[member * NBLK + b, :total, :],
                        (((1,), (1,)), ((), ())),
                        preferred_element_type=jnp.float32,
                    )
                )
            pos = lax.rem(lax.broadcasted_iota(jnp.int32, (rows, block), 0), block)
            causal = lax.broadcasted_iota(jnp.int32, (rows, block), 1) <= pos
            for member, (total, scores) in enumerate(zip(totals, all_scores)):
                col = lax.broadcasted_iota(jnp.int32, (1, total - block), 1) + block
                bias = jnp.where(col < counts[member], 0.0, neg_big)
                first = jnp.where(causal, scores[:, :block] * score_scale, neg_big)
                rest = scores[:, block:] * score_scale + bias
                most_score = jnp.maximum(
                    jnp.max(first, axis=1, keepdims=True), jnp.max(rest, axis=1, keepdims=True)
                )
                weights = jnp.exp2(jnp.concatenate([first, rest], axis=1) - most_score)
                part_ref[member] = 1.0 / jnp.sum(weights, axis=1, keepdims=True)
                total_ref[member] = lax.dot_general(
                    weights.astype(jnp.bfloat16),
                    near[member * NBLK + b, :total, :lat],
                    (((1,), (0,)), ((), ())),
                    preferred_element_type=jnp.float32,
                )

        ends = range(TILE, most + 1, TILE)
        needs = counts
        choices = list(itertools.product(ends, repeat=cpg))
        if len(choices) > MOST_BODIES:
            needs = [functools.reduce(jnp.maximum, counts)] * cpg
            choices = [(total,) * cpg for total in ends]
        for totals in choices:
            fits = functools.reduce(
                jnp.logical_and,
                [jnp.logical_and(n > total - TILE, n <= total) for n, total in zip(needs, totals)],
            )
            pl.when(fits)(functools.partial(attend, totals))

        @pl.when(b >= 1)
        def _():
            for member in range(cpg):
                out_copy(b - 1, member, slot).start()

        return 0

    lax.fori_loop(0, NBLK, step, 0)
    last = (NBLK + 1) % 2
    for member in range(cpg):
        out_copy(NBLK - 3, member, last).wait()
    put(last)
    for member in range(cpg):
        out_copy(NBLK - 1, member, last).start()
    for member in range(cpg):
        out_copy(NBLK - 2, member, 1 - last).wait()
        out_copy(NBLK - 1, member, last).wait()


def shards(queries, keys, block_mask, summary_start):
    row_total, head_count, key_width = queries.shape
    lat_width = key_width - ROPE
    seq_count = lax.axis_size("seq")
    total_cands = block_mask.shape[0]
    cpg = total_cands // seq_count
    seq_len = row_total // cpg
    block_len = seq_len // NBLK
    summ_len = block_len // 2
    most = NBLK * block_len + (total_cands - 1) * summ_len
    most = -(-most // TILE) * TILE
    vmem = pl.BlockSpec(memory_space=pltpu.VMEM)
    smem = pl.BlockSpec(memory_space=pltpu.SMEM)

    held, other, by_head = gather_steps(keys, queries)
    first, second = step_orders(lax.axis_size("exp"))
    own = pl.pallas_call(
        functools.partial(pick_kernel, cpg, (first, second)),
        out_shape=jax.ShapeDtypeStruct((cpg * summ_len, key_width), keys.dtype),
        in_specs=[smem, vmem, vmem],
        out_specs=vmem,
        compiler_params=grant(2),
        name="pick",
    )(summary_start, held, other)
    ordered = pl.pallas_call(
        functools.partial(order_kernel, slot_offsets(first), slot_offsets(second)),
        out_shape=jax.ShapeDtypeStruct((row_total, key_width), keys.dtype),
        in_specs=[vmem, vmem],
        out_specs=vmem,
        compiler_params=grant(2),
        cost_estimate=pl.CostEstimate(flops=10**9, bytes_accessed=0, transcendentals=0),
        name="order",
    )(held, other)
    dims = (head_count, cpg, total_cands, seq_len, block_len, summ_len, lat_width)
    near_rows = NBLK * block_len + (total_cands - 1) * summ_len + TILE
    near = pl.pallas_call(
        functools.partial(prepare_kernel, dims),
        out_shape=jax.ShapeDtypeStruct((cpg * NBLK, near_rows, key_width), keys.dtype),
        in_specs=[smem, vmem, vmem],
        out_specs=vmem,
        compiler_params=grant(2),
        cost_estimate=pl.CostEstimate(flops=10**9, bytes_accessed=0, transcendentals=0),
        name="prepare",
    )(block_mask, ordered, own)
    sums = own
    bit = 1
    while bit < seq_count:
        pairs = [(i, i ^ bit) for i in range(seq_count)]
        got = lax.ppermute(sums, "seq", pairs)
        if 2 * bit >= seq_count:
            got, near = lax.optimization_barrier((got, near))
        sums = join(sums, got)
        bit *= 2
    rows = head_count * block_len
    return pl.pallas_call(
        functools.partial(attend_kernel, dims, most),
        out_shape=[
            jax.ShapeDtypeStruct((row_total, head_count, lat_width), queries.dtype),
            jax.ShapeDtypeStruct(near.shape, near.dtype),
        ],
        in_specs=[smem, vmem, vmem] + [vmem] * len(by_head),
        out_specs=[pl.BlockSpec(memory_space=pl.ANY), vmem],
        scratch_shapes=[
            pltpu.VMEM((cpg, rows, lat_width), jnp.float32),
            pltpu.VMEM((cpg, rows, 1), jnp.float32),
            pltpu.VMEM((2, cpg, block_len, head_count, lat_width), queries.dtype),
            pltpu.SemaphoreType.DMA((2, cpg)),
        ],
        input_output_aliases={1: 1},
        compiler_params=grant(20),
        name="attend",
    )(block_mask, near, sums, *by_head)[0]


def solution(mesh):
    placed = (P("seq", "exp", None), P(("seq", "exp"), None), P(), P())
    return jax.shard_map(
        shards, mesh=mesh, in_specs=placed, out_specs=P("seq", "exp", None), check_vma=False
    )
```

```python
import functools
import itertools
import math

import jax
import jax.numpy as jnp
from jax import lax
from jax.experimental import pallas as pl
from jax.experimental.pallas import tpu as pltpu
from jax.sharding import PartitionSpec as P

ROPE = 64
NBLK = 4
TILE = 256
MOST_BODIES = 9

score_scale = 192.0 ** (-0.5) * math.log2(math.e)
neg_big = -1e30


def step_orders(count):
    bits = [1 << k for k in range(1, count.bit_length() - 1)]
    bits.reverse()
    first = bits[:1] + bits[:0:-1]
    return first, first[-1:] + first[:-1]


def slot_offsets(order):
    offsets = [0]
    for bit in order:
        offsets = offsets + [o ^ bit for o in offsets]
    return offsets


def grant(mib):
    return pltpu.CompilerParams(vmem_limit_bytes=mib << 20)


def join_kernel(first_ref, second_ref, out_ref):
    half = first_ref.shape[0]
    out_ref[:half] = first_ref[...]
    out_ref[half:] = second_ref[...]


def join(first, second):
    vmem = pl.BlockSpec(memory_space=pltpu.VMEM)
    return pl.pallas_call(
        join_kernel,
        out_shape=jax.ShapeDtypeStruct((2 * first.shape[0],) + first.shape[1:], first.dtype),
        in_specs=[vmem, vmem],
        out_specs=vmem,
        compiler_params=grant(2),
        name="join",
    )(first, second)


def keep_kernel(in_ref, out_ref):
    out_ref[...] = in_ref[...]


def keep(array):
    vmem = pl.BlockSpec(memory_space=pltpu.VMEM)
    return pl.pallas_call(
        keep_kernel,
        out_shape=jax.ShapeDtypeStruct(array.shape, array.dtype),
        in_specs=[vmem],
        out_specs=vmem,
        compiler_params=grant(2),
        name="keep",
    )(array)


def turn_kernel(in_ref, out_ref):
    for h in range(in_ref.shape[0]):
        out_ref[h] = in_ref[h].T


def turn(by_width, head, total):
    _, width, rows = by_width.shape
    cut = min(rows, 256)
    return pl.pallas_call(
        turn_kernel,
        out_shape=jax.ShapeDtypeStruct((total, rows, width), by_width.dtype),
        grid=(total, rows // cut),
        in_specs=[pl.BlockSpec((1, width, cut), lambda h, i: (head + h, 0, i))],
        out_specs=pl.BlockSpec((1, cut, width), lambda h, i: (h, i, 0)),
        compiler_params=grant(4),
        name="turn",
    )(by_width)


def gather_steps(keys, queries):
    count = lax.axis_size("exp")
    heads = queries.shape[1]
    first, second = step_orders(count)
    last = len(first)
    by_width = jnp.transpose(queries, (1, 2, 0))
    swap = [(i, i ^ 1) for i in range(count)]
    by_head = []
    done = 0
    held = keys[None]
    for k, (bit_a, bit_b) in enumerate(zip(first, second)):
        pairs = [(i, i ^ (bit_b if i & 1 else bit_a)) for i in range(count)]
        got = lax.ppermute(held, "exp", pairs)
        if k == 0:
            got, held = lax.optimization_barrier((got, keep(held)))
        due = heads if k == last - 1 else heads * k // (2 * (last - 1))
        if k == last - 1:
            other = lax.ppermute(held, "exp", swap)
            got, other = lax.optimization_barrier((got, other))
        if due > done:
            piece = turn(by_width, done, due - done)
            got, piece = lax.optimization_barrier((got, piece))
            by_head.append(piece)
            done = due
        if k < last - 1:
            held = join(held, got)
    return (held, got), (other, lax.ppermute(got, "exp", swap)), by_head


def pick_kernel(cpg, orders, start_ref, *refs):
    buffers, own_ref = refs[:-1], refs[-1]
    me = lax.axis_index("exp")
    group = lax.axis_index("seq")
    half, shard, _ = buffers[0].shape
    summ = own_ref.shape[0] // cpg
    length = 4 * half * shard // cpg
    piece = min(shard, summ)
    starts = start_ref[...].astype(jnp.float32)
    cands = lax.broadcasted_iota(jnp.int32, starts.shape, 1)
    for member in range(cpg):
        start = jnp.sum(jnp.where(cands == group * cpg + member, starts, 0.0)).astype(jnp.int32)
        for k in range(summ // piece):
            row = member * length + start + k * piece
            owner = row // shard
            inside = pl.multiple_of(lax.rem(row, shard), piece)
            slots = [
                sum(((owner ^ me) // bit % 2) << place for place, bit in enumerate(order))
                for order in orders
            ]
            part = owner % 2
            slot = jnp.where(part == 0, slots[0], slots[1])
            buffer = jnp.where(part == me % 2, 0, 2) + slot // half
            at = slice(member * summ + k * piece, member * summ + (k + 1) * piece)
            for number, ref in enumerate(buffers):

                @pl.when(buffer == number)
                def _():
                    own_ref[at, :] = ref[lax.rem(slot, half), pl.ds(inside, piece), :]


def order_kernel(offsets_a, offsets_b, *refs):
    buffers, keys_ref = refs[:-1], refs[-1]
    me = lax.axis_index("exp")
    part = me % 2
    half, shard, _ = buffers[0].shape
    for s, (a, b) in enumerate(zip(offsets_a, offsets_b)):
        here = (me ^ jnp.where(part == 0, a, b)) * shard
        there = (me ^ 1 ^ jnp.where(part == 0, b, a)) * shard
        for target, ref in ((here, buffers[s // half]), (there, buffers[2 + s // half])):
            keys_ref[pl.ds(pl.multiple_of(target, shard), shard), :] = ref[s % half]


def prepare_kernel(dims, mask_ref, keys_ref, own_ref, near_ref):
    heads, cpg, cands, length, block, summ, lat = dims
    group = lax.axis_index("seq")
    tail = (cands - cpg) * summ + TILE

    def step(i, _):
        member, b = i // NBLK, lax.rem(i, NBLK)
        cand = group * cpg + member
        near_ref[i, 0:block, :] = keys_ref[pl.ds(pl.multiple_of(i * block, block), block), :]
        n = jnp.int32(block)
        for j in range(NBLK - 1):
            seen = jnp.logical_and(j < b, mask_ref[cand, b, j] == 1)

            @pl.when(seen)
            def _():
                near_ref[i, pl.ds(pl.multiple_of(n, summ), block), :] = keys_ref[
                    pl.ds(pl.multiple_of(member * length + j * block, block), block), :
                ]

            n = n + jnp.where(seen, block, 0)
        for d in range(cpg):
            seen = mask_ref[cand, b, NBLK + group * cpg + d] == 1

            @pl.when(seen)
            def _():
                near_ref[i, pl.ds(pl.multiple_of(n, summ), summ), :] = own_ref[
                    d * summ : (d + 1) * summ, :
                ]

            n = n + jnp.where(seen, summ, 0)
        near_ref[i, pl.ds(pl.multiple_of(n, summ), tail), :] = jnp.zeros(
            (tail, near_ref.shape[2]), near_ref.dtype
        )
        return 0

    lax.fori_loop(0, cpg * NBLK, step, 0)


def attend_kernel(dims, most, mask_ref, got_ref, sums_ref, *refs):
    heads, cpg, cands, length, block, summ, lat = dims
    q_refs, (out_ref, near, total_ref, part_ref, staged, sem) = refs[:-6], refs[-6:]
    group = lax.axis_index("seq")
    rows = heads * block

    def out_copy(b, member, slot):
        at = pl.ds(pl.multiple_of(member * length + b * block, block), block)
        return pltpu.make_async_copy(
            staged.at[slot, member], out_ref.at[at], sem.at[slot, member]
        )

    def put(slot):
        for member in range(cpg):
            result = (total_ref[member] * part_ref[member]).astype(jnp.bfloat16)
            staged[slot, member] = jnp.swapaxes(result.reshape(heads, block, lat), 0, 1)

    def add_seen(b, member):
        cand = group * cpg + member
        n = jnp.int32(block)
        for j in range(NBLK - 1):
            n = n + jnp.where(jnp.logical_and(j < b, mask_ref[cand, b, j] == 1), block, 0)
        for d in range(cpg):
            n = n + jnp.where(mask_ref[cand, b, NBLK + group * cpg + d] == 1, summ, 0)
        for d in range(cands):
            seen = jnp.logical_and(mask_ref[cand, b, NBLK + d] == 1, d // cpg != group)
            row = ((group ^ (d // cpg)) * cpg + d % cpg) * summ

            @pl.when(seen)
            def _():
                near[member * NBLK + b, pl.ds(pl.multiple_of(n, summ), summ), :] = sums_ref[
                    pl.ds(pl.multiple_of(row, summ), summ), :
                ]

            n = n + jnp.where(seen, summ, 0)
        return n

    def step(b, _):
        slot = lax.rem(b + 1, 2)
        counts = [add_seen(b, member) for member in range(cpg)]

        @pl.when(b >= 3)
        def _():
            for member in range(cpg):
                out_copy(b - 3, member, slot).wait()

        def attend(totals):
            put(slot)
            all_scores = []
            for member, total in enumerate(totals):
                at = pl.ds(pl.multiple_of(member * length + b * block, block), block)
                q = jnp.concatenate(
                    [q_ref[h, at, :] for q_ref in q_refs for h in range(q_ref.shape[0])], axis=0
                )
                all_scores.append(
                    lax.dot_general(
                        q,
                        near[member * NBLK + b, :total, :],
                        (((1,), (1,)), ((), ())),
                        preferred_element_type=jnp.float32,
                    )
                )
            pos = lax.rem(lax.broadcasted_iota(jnp.int32, (rows, block), 0), block)
            causal = lax.broadcasted_iota(jnp.int32, (rows, block), 1) <= pos
            for member, (total, scores) in enumerate(zip(totals, all_scores)):
                col = lax.broadcasted_iota(jnp.int32, (1, total - block), 1) + block
                bias = jnp.where(col < counts[member], 0.0, neg_big)
                first = jnp.where(causal, scores[:, :block] * score_scale, neg_big)
                rest = scores[:, block:] * score_scale + bias
                most_score = jnp.maximum(
                    jnp.max(first, axis=1, keepdims=True), jnp.max(rest, axis=1, keepdims=True)
                )
                weights = jnp.exp2(jnp.concatenate([first, rest], axis=1) - most_score)
                part_ref[member] = 1.0 / jnp.sum(weights, axis=1, keepdims=True)
                total_ref[member] = lax.dot_general(
                    weights.astype(jnp.bfloat16),
                    near[member * NBLK + b, :total, :lat],
                    (((1,), (0,)), ((), ())),
                    preferred_element_type=jnp.float32,
                )

        ends = range(TILE, most + 1, TILE)
        needs = counts
        choices = list(itertools.product(ends, repeat=cpg))
        if len(choices) > MOST_BODIES:
            needs = [functools.reduce(jnp.maximum, counts)] * cpg
            choices = [(total,) * cpg for total in ends]
        for totals in choices:
            fits = functools.reduce(
                jnp.logical_and,
                [jnp.logical_and(n > total - TILE, n <= total) for n, total in zip(needs, totals)],
            )
            pl.when(fits)(functools.partial(attend, totals))

        @pl.when(b >= 1)
        def _():
            for member in range(cpg):
                out_copy(b - 1, member, slot).start()

        return 0

    lax.fori_loop(0, NBLK, step, 0)
    last = (NBLK + 1) % 2
    for member in range(cpg):
        out_copy(NBLK - 3, member, last).wait()
    put(last)
    for member in range(cpg):
        out_copy(NBLK - 1, member, last).start()
    for member in range(cpg):
        out_copy(NBLK - 2, member, 1 - last).wait()
        out_copy(NBLK - 1, member, last).wait()


def shards(queries, keys, block_mask, summary_start):
    row_total, head_count, key_width = queries.shape
    lat_width = key_width - ROPE
    seq_count = lax.axis_size("seq")
    total_cands = block_mask.shape[0]
    cpg = total_cands // seq_count
    seq_len = row_total // cpg
    block_len = seq_len // NBLK
    summ_len = block_len // 2
    most = NBLK * block_len + (total_cands - 1) * summ_len
    most = -(-most // TILE) * TILE
    vmem = pl.BlockSpec(memory_space=pltpu.VMEM)
    smem = pl.BlockSpec(memory_space=pltpu.SMEM)

    held, other, by_head = gather_steps(keys, queries)
    first, second = step_orders(lax.axis_size("exp"))
    own = pl.pallas_call(
        functools.partial(pick_kernel, cpg, (first, second)),
        out_shape=jax.ShapeDtypeStruct((cpg * summ_len, key_width), keys.dtype),
        in_specs=[vmem] * 5,
        out_specs=vmem,
        compiler_params=grant(2),
        name="pick",
    )(summary_start.reshape(1, -1), *held, *other)
    ordered = pl.pallas_call(
        functools.partial(order_kernel, slot_offsets(first), slot_offsets(second)),
        out_shape=jax.ShapeDtypeStruct((row_total, key_width), keys.dtype),
        in_specs=[vmem] * 4,
        out_specs=vmem,
        compiler_params=grant(2),
        cost_estimate=pl.CostEstimate(flops=10**9, bytes_accessed=0, transcendentals=0),
        name="order",
    )(*held, *other)
    dims = (head_count, cpg, total_cands, seq_len, block_len, summ_len, lat_width)
    near_rows = NBLK * block_len + (total_cands - 1) * summ_len + TILE
    near = pl.pallas_call(
        functools.partial(prepare_kernel, dims),
        out_shape=jax.ShapeDtypeStruct((cpg * NBLK, near_rows, key_width), keys.dtype),
        in_specs=[smem, vmem, vmem],
        out_specs=vmem,
        compiler_params=grant(2),
        cost_estimate=pl.CostEstimate(flops=10**9, bytes_accessed=0, transcendentals=0),
        name="prepare",
    )(block_mask, ordered, own)
    sums = own
    bit = 1
    while bit < seq_count:
        pairs = [(i, i ^ bit) for i in range(seq_count)]
        got = lax.ppermute(sums, "seq", pairs)
        if 2 * bit >= seq_count:
            got, near = lax.optimization_barrier((got, near))
        sums = join(sums, got)
        bit *= 2
    rows = head_count * block_len
    return pl.pallas_call(
        functools.partial(attend_kernel, dims, most),
        out_shape=[
            jax.ShapeDtypeStruct((row_total, head_count, lat_width), queries.dtype),
            jax.ShapeDtypeStruct(near.shape, near.dtype),
        ],
        in_specs=[smem, vmem, vmem] + [vmem] * len(by_head),
        out_specs=[pl.BlockSpec(memory_space=pl.ANY), vmem],
        scratch_shapes=[
            pltpu.VMEM((cpg, rows, lat_width), jnp.float32),
            pltpu.VMEM((cpg, rows, 1), jnp.float32),
            pltpu.VMEM((2, cpg, block_len, head_count, lat_width), queries.dtype),
            pltpu.SemaphoreType.DMA((2, cpg)),
        ],
        input_output_aliases={1: 1},
        compiler_params=grant(20),
        name="attend",
    )(block_mask, near, sums, *by_head)[0]


def solution(mesh):
    placed = (P("seq", "exp", None), P(("seq", "exp"), None), P(), P())
    return jax.shard_map(
        shards, mesh=mesh, in_specs=placed, out_specs=P("seq", "exp", None), check_vma=False
    )
```

```python
import functools
import itertools
import math

import jax
import jax.numpy as jnp
from jax import lax
from jax.experimental import pallas as pl
from jax.experimental.pallas import tpu as pltpu
from jax.sharding import PartitionSpec as P

ROPE = 64
NBLK = 4
TILE = 256
MOST_BODIES = 9

score_scale = 192.0 ** (-0.5) * math.log2(math.e)
neg_big = -1e30


def step_orders(count):
    bits = [1 << k for k in range(1, count.bit_length() - 1)]
    bits.reverse()
    first = bits[:1] + bits[:0:-1]
    return first, first[-1:] + first[:-1]


def slot_offsets(order):
    offsets = [0]
    for bit in order:
        offsets = offsets + [o ^ bit for o in offsets]
    return offsets


def grant(mib):
    return pltpu.CompilerParams(vmem_limit_bytes=mib << 20)


def join_kernel(first_ref, second_ref, out_ref):
    half = first_ref.shape[0]
    out_ref[:half] = first_ref[...]
    out_ref[half:] = second_ref[...]


def join(first, second):
    vmem = pl.BlockSpec(memory_space=pltpu.VMEM)
    return pl.pallas_call(
        join_kernel,
        out_shape=jax.ShapeDtypeStruct((2 * first.shape[0],) + first.shape[1:], first.dtype),
        in_specs=[vmem, vmem],
        out_specs=vmem,
        compiler_params=grant(2),
        name="join",
    )(first, second)


def keep_kernel(in_ref, out_ref):
    out_ref[...] = in_ref[...]


def keep(array):
    vmem = pl.BlockSpec(memory_space=pltpu.VMEM)
    return pl.pallas_call(
        keep_kernel,
        out_shape=jax.ShapeDtypeStruct(array.shape, array.dtype),
        in_specs=[vmem],
        out_specs=vmem,
        compiler_params=grant(2),
        name="keep",
    )(array)


def turn_kernel(in_ref, out_ref):
    for h in range(in_ref.shape[0]):
        out_ref[h] = in_ref[h].T


def turn(by_width, head, total):
    _, width, rows = by_width.shape
    cut = min(rows, 256)
    return pl.pallas_call(
        turn_kernel,
        out_shape=jax.ShapeDtypeStruct((total, rows, width), by_width.dtype),
        grid=(total, rows // cut),
        in_specs=[pl.BlockSpec((1, width, cut), lambda h, i: (head + h, 0, i))],
        out_specs=pl.BlockSpec((1, cut, width), lambda h, i: (h, i, 0)),
        compiler_params=grant(4),
        name="turn",
    )(by_width)


def gather_steps(keys, queries):
    count = lax.axis_size("exp")
    heads = queries.shape[1]
    first, second = step_orders(count)
    last = len(first)
    by_width = jnp.transpose(queries, (1, 2, 0))
    swap = [(i, i ^ 1) for i in range(count)]
    by_head = []
    done = 0
    held = keys[None]
    for k, (bit_a, bit_b) in enumerate(zip(first, second)):
        pairs = [(i, i ^ (bit_b if i & 1 else bit_a)) for i in range(count)]
        got = lax.ppermute(held, "exp", pairs)
        if k == 0:
            got, held = lax.optimization_barrier((got, keep(held)))
        due = heads if k == last - 1 else heads * k // (2 * (last - 1))
        if k == last - 1:
            other = lax.ppermute(held, "exp", swap)
            got, other = lax.optimization_barrier((got, other))
        if due > done:
            piece = turn(by_width, done, due - done)
            got, piece = lax.optimization_barrier((got, piece))
            by_head.append(piece)
            done = due
        if k < last - 1:
            held = join(held, got)
    return (held, got), (other, lax.ppermute(got, "exp", swap)), by_head


def pick_kernel(cpg, orders, start_ref, *refs):
    buffers, own_ref = refs[:-1], refs[-1]
    me = lax.axis_index("exp")
    group = lax.axis_index("seq")
    half, shard, _ = buffers[0].shape
    summ = own_ref.shape[0] // cpg
    length = 4 * half * shard // cpg
    piece = min(shard, summ)
    starts = start_ref[...].astype(jnp.float32)
    cands = lax.broadcasted_iota(jnp.int32, starts.shape, 1)
    for member in range(cpg):
        start = jnp.sum(jnp.where(cands == group * cpg + member, starts, 0.0)).astype(jnp.int32)
        for k in range(summ // piece):
            row = member * length + start + k * piece
            owner = row // shard
            inside = pl.multiple_of(lax.rem(row, shard), piece)
            slots = [
                sum(((owner ^ me) // bit % 2) << place for place, bit in enumerate(order))
                for order in orders
            ]
            part = owner % 2
            slot = jnp.where(part == 0, slots[0], slots[1])
            buffer = jnp.where(part == me % 2, 0, 2) + slot // half
            at = slice(member * summ + k * piece, member * summ + (k + 1) * piece)
            for number, ref in enumerate(buffers):

                @pl.when(buffer == number)
                def _():
                    own_ref[at, :] = ref[lax.rem(slot, half), pl.ds(inside, piece), :]


def half_kernel(own_ref, out_ref):
    part = lax.axis_index("exp") % 2
    summ = out_ref.shape[0]
    out_ref[...] = own_ref[pl.ds(pl.multiple_of(part * summ, summ), summ), :]


def both_kernel(own_ref, got_ref, rest_ref, out_ref):
    part = lax.axis_index("exp") % 2
    summ = got_ref.shape[0]
    out_ref[: 2 * summ, :] = own_ref[...]
    out_ref[pl.ds(pl.multiple_of((2 + part) * summ, summ), summ), :] = got_ref[...]
    out_ref[pl.ds(pl.multiple_of((3 - part) * summ, summ), summ), :] = rest_ref[...]


def order_kernel(offsets_a, offsets_b, *refs):
    buffers, keys_ref = refs[:-1], refs[-1]
    me = lax.axis_index("exp")
    part = me % 2
    half, shard, _ = buffers[0].shape
    for s, (a, b) in enumerate(zip(offsets_a, offsets_b)):
        here = (me ^ jnp.where(part == 0, a, b)) * shard
        there = (me ^ 1 ^ jnp.where(part == 0, b, a)) * shard
        for target, ref in ((here, buffers[s // half]), (there, buffers[2 + s // half])):
            keys_ref[pl.ds(pl.multiple_of(target, shard), shard), :] = ref[s % half]


def prepare_kernel(dims, mask_ref, keys_ref, own_ref, near_ref):
    heads, cpg, cands, length, block, summ, lat = dims
    group = lax.axis_index("seq")
    tail = (cands - cpg) * summ + TILE

    def step(i, _):
        member, b = i // NBLK, lax.rem(i, NBLK)
        cand = group * cpg + member
        near_ref[i, 0:block, :] = keys_ref[pl.ds(pl.multiple_of(i * block, block), block), :]
        n = jnp.int32(block)
        for j in range(NBLK - 1):
            seen = jnp.logical_and(j < b, mask_ref[cand, b, j] == 1)

            @pl.when(seen)
            def _():
                near_ref[i, pl.ds(pl.multiple_of(n, summ), block), :] = keys_ref[
                    pl.ds(pl.multiple_of(member * length + j * block, block), block), :
                ]

            n = n + jnp.where(seen, block, 0)
        for d in range(cpg):
            seen = mask_ref[cand, b, NBLK + group * cpg + d] == 1

            @pl.when(seen)
            def _():
                near_ref[i, pl.ds(pl.multiple_of(n, summ), summ), :] = own_ref[
                    d * summ : (d + 1) * summ, :
                ]

            n = n + jnp.where(seen, summ, 0)
        near_ref[i, pl.ds(pl.multiple_of(n, summ), tail), :] = jnp.zeros(
            (tail, near_ref.shape[2]), near_ref.dtype
        )
        return 0

    lax.fori_loop(0, cpg * NBLK, step, 0)


def attend_kernel(dims, most, mask_ref, got_ref, sums_ref, *refs):
    heads, cpg, cands, length, block, summ, lat = dims
    q_refs, (out_ref, near, total_ref, part_ref, staged, sem) = refs[:-6], refs[-6:]
    group = lax.axis_index("seq")
    rows = heads * block

    def out_copy(b, member, slot):
        at = pl.ds(pl.multiple_of(member * length + b * block, block), block)
        return pltpu.make_async_copy(
            staged.at[slot, member], out_ref.at[at], sem.at[slot, member]
        )

    def put(slot):
        for member in range(cpg):
            result = (total_ref[member] * part_ref[member]).astype(jnp.bfloat16)
            staged[slot, member] = jnp.swapaxes(result.reshape(heads, block, lat), 0, 1)

    def add_seen(b, member):
        cand = group * cpg + member
        n = jnp.int32(block)
        for j in range(NBLK - 1):
            n = n + jnp.where(jnp.logical_and(j < b, mask_ref[cand, b, j] == 1), block, 0)
        for d in range(cpg):
            n = n + jnp.where(mask_ref[cand, b, NBLK + group * cpg + d] == 1, summ, 0)
        for d in range(cands):
            seen = jnp.logical_and(mask_ref[cand, b, NBLK + d] == 1, d // cpg != group)
            row = ((group ^ (d // cpg)) * cpg + d % cpg) * summ

            @pl.when(seen)
            def _():
                near[member * NBLK + b, pl.ds(pl.multiple_of(n, summ), summ), :] = sums_ref[
                    pl.ds(pl.multiple_of(row, summ), summ), :
                ]

            n = n + jnp.where(seen, summ, 0)
        return n

    def step(b, _):
        slot = lax.rem(b + 1, 2)
        counts = [add_seen(b, member) for member in range(cpg)]

        @pl.when(b >= 3)
        def _():
            for member in range(cpg):
                out_copy(b - 3, member, slot).wait()

        def attend(totals):
            put(slot)
            all_scores = []
            for member, total in enumerate(totals):
                at = pl.ds(pl.multiple_of(member * length + b * block, block), block)
                q = jnp.concatenate(
                    [q_ref[h, at, :] for q_ref in q_refs for h in range(q_ref.shape[0])], axis=0
                )
                all_scores.append(
                    lax.dot_general(
                        q,
                        near[member * NBLK + b, :total, :],
                        (((1,), (1,)), ((), ())),
                        preferred_element_type=jnp.float32,
                    )
                )
            pos = lax.rem(lax.broadcasted_iota(jnp.int32, (rows, block), 0), block)
            causal = lax.broadcasted_iota(jnp.int32, (rows, block), 1) <= pos
            for member, (total, scores) in enumerate(zip(totals, all_scores)):
                col = lax.broadcasted_iota(jnp.int32, (1, total - block), 1) + block
                bias = jnp.where(col < counts[member], 0.0, neg_big)
                first = jnp.where(causal, scores[:, :block] * score_scale, neg_big)
                rest = scores[:, block:] * score_scale + bias
                most_score = jnp.maximum(
                    jnp.max(first, axis=1, keepdims=True), jnp.max(rest, axis=1, keepdims=True)
                )
                weights = jnp.exp2(jnp.concatenate([first, rest], axis=1) - most_score)
                part_ref[member] = 1.0 / jnp.sum(weights, axis=1, keepdims=True)
                total_ref[member] = lax.dot_general(
                    weights.astype(jnp.bfloat16),
                    near[member * NBLK + b, :total, :lat],
                    (((1,), (0,)), ((), ())),
                    preferred_element_type=jnp.float32,
                )

        ends = range(TILE, most + 1, TILE)
        needs = counts
        choices = list(itertools.product(ends, repeat=cpg))
        if len(choices) > MOST_BODIES:
            needs = [functools.reduce(jnp.maximum, counts)] * cpg
            choices = [(total,) * cpg for total in ends]
        for totals in choices:
            fits = functools.reduce(
                jnp.logical_and,
                [jnp.logical_and(n > total - TILE, n <= total) for n, total in zip(needs, totals)],
            )
            pl.when(fits)(functools.partial(attend, totals))

        @pl.when(b >= 1)
        def _():
            for member in range(cpg):
                out_copy(b - 1, member, slot).start()

        return 0

    lax.fori_loop(0, NBLK, step, 0)
    last = (NBLK + 1) % 2
    for member in range(cpg):
        out_copy(NBLK - 3, member, last).wait()
    put(last)
    for member in range(cpg):
        out_copy(NBLK - 1, member, last).start()
    for member in range(cpg):
        out_copy(NBLK - 2, member, 1 - last).wait()
        out_copy(NBLK - 1, member, last).wait()


def shards(queries, keys, block_mask, summary_start):
    row_total, head_count, key_width = queries.shape
    lat_width = key_width - ROPE
    seq_count = lax.axis_size("seq")
    total_cands = block_mask.shape[0]
    cpg = total_cands // seq_count
    seq_len = row_total // cpg
    block_len = seq_len // NBLK
    summ_len = block_len // 2
    most = NBLK * block_len + (total_cands - 1) * summ_len
    most = -(-most // TILE) * TILE
    vmem = pl.BlockSpec(memory_space=pltpu.VMEM)
    smem = pl.BlockSpec(memory_space=pltpu.SMEM)

    held, other, by_head = gather_steps(keys, queries)
    first, second = step_orders(lax.axis_size("exp"))
    own = pl.pallas_call(
        functools.partial(pick_kernel, cpg, (first, second)),
        out_shape=jax.ShapeDtypeStruct((cpg * summ_len, key_width), keys.dtype),
        in_specs=[vmem] * 5,
        out_specs=vmem,
        compiler_params=grant(2),
        name="pick",
    )(summary_start.reshape(1, -1), *held, *other)
    ordered = pl.pallas_call(
        functools.partial(order_kernel, slot_offsets(first), slot_offsets(second)),
        out_shape=jax.ShapeDtypeStruct((row_total, key_width), keys.dtype),
        in_specs=[vmem] * 4,
        out_specs=vmem,
        compiler_params=grant(2),
        cost_estimate=pl.CostEstimate(flops=10**9, bytes_accessed=0, transcendentals=0),
        name="order",
    )(*held, *other)
    dims = (head_count, cpg, total_cands, seq_len, block_len, summ_len, lat_width)
    near_rows = NBLK * block_len + (total_cands - 1) * summ_len + TILE
    near = pl.pallas_call(
        functools.partial(prepare_kernel, dims),
        out_shape=jax.ShapeDtypeStruct((cpg * NBLK, near_rows, key_width), keys.dtype),
        in_specs=[smem, vmem, vmem],
        out_specs=vmem,
        compiler_params=grant(2),
        cost_estimate=pl.CostEstimate(flops=10**9, bytes_accessed=0, transcendentals=0),
        name="prepare",
    )(block_mask, ordered, own)
    sums = own
    bit = 1
    if seq_count == 2 and cpg == 2:
        mine = pl.pallas_call(
            half_kernel,
            out_shape=jax.ShapeDtypeStruct((summ_len, key_width), keys.dtype),
            in_specs=[vmem],
            out_specs=vmem,
            compiler_params=grant(2),
            name="half",
        )(own)
        got = lax.ppermute(mine, "seq", [(0, 1), (1, 0)])
        got, near = lax.optimization_barrier((got, near))
        exp_count = lax.axis_size("exp")
        rest = lax.ppermute(got, "exp", [(i, i ^ 1) for i in range(exp_count)])
        sums = pl.pallas_call(
            both_kernel,
            out_shape=jax.ShapeDtypeStruct((4 * summ_len, key_width), keys.dtype),
            in_specs=[vmem] * 3,
            out_specs=vmem,
            compiler_params=grant(2),
            name="both",
        )(own, got, rest)
        bit = seq_count
    while bit < seq_count:
        pairs = [(i, i ^ bit) for i in range(seq_count)]
        got = lax.ppermute(sums, "seq", pairs)
        if 2 * bit >= seq_count:
            got, near = lax.optimization_barrier((got, near))
        sums = join(sums, got)
        bit *= 2
    rows = head_count * block_len
    return pl.pallas_call(
        functools.partial(attend_kernel, dims, most),
        out_shape=[
            jax.ShapeDtypeStruct((row_total, head_count, lat_width), queries.dtype),
            jax.ShapeDtypeStruct(near.shape, near.dtype),
        ],
        in_specs=[smem, vmem, vmem] + [vmem] * len(by_head),
        out_specs=[pl.BlockSpec(memory_space=pl.ANY), vmem],
        scratch_shapes=[
            pltpu.VMEM((cpg, rows, lat_width), jnp.float32),
            pltpu.VMEM((cpg, rows, 1), jnp.float32),
            pltpu.VMEM((2, cpg, block_len, head_count, lat_width), queries.dtype),
            pltpu.SemaphoreType.DMA((2, cpg)),
        ],
        input_output_aliases={1: 1},
        compiler_params=grant(20),
        name="attend",
    )(block_mask, near, sums, *by_head)[0]


def solution(mesh):
    placed = (P("seq", "exp", None), P(("seq", "exp"), None), P(), P())
    return jax.shard_map(
        shards, mesh=mesh, in_specs=placed, out_specs=P("seq", "exp", None), check_vma=False
    )
```
